32 devices in a mesh: parts: 2 (over x), space: 16 (over z, y, core).
Axes of the slice: x: 2, y: 2, z: 4, core: 2. Of those that a mesh axis runs over, the one named last changes fastest.
Arguments:
- volume: bfloat16 [64, 16, 16, 128], P(('parts', 'space')), parts along dimension 0, may hold values from -6 to 6
- first_filter: bfloat16 [3, 3, 3, 128, 128], replicated, may hold values from -0.109375 to 0.109375
- second_filter: bfloat16 [3, 3, 3, 128, 128], replicated, may hold values from -0.109375 to 0.109375
- cotangent: bfloat16 [64, 16, 16, 128], P(('parts', 'space')), parts along dimension 0, may hold values from -0.06591797 to 0.06591797
Outputs:
- response: bfloat16 [64, 16, 16, 128], P(('parts', 'space')), parts along dimension 0
- first_grad: float32 [256, 3, 3, 3, 128], P(('parts', 'space')), parts along dimension 0
- second_grad: float32 [256, 3, 3, 3, 128], P(('parts', 'space')), parts along dimension 0
The draws below stay inside these ranges and needn't reach their ends.
There are 2 independent parts, one for each index of `parts`. The reference program is written for one: setup_inputs(seed, part) draws one part's arguments, and reference() takes and returns one part's arrays. A program takes and returns all parts, laid end to end along the dimension named above; an argument that names none is the same for every part. Nothing has to cross between parts.
All inputs are finite; a program needn't handle non-finite values.
Results may differ from the reference program's by a relative error of at most 0.0049.
Values may be sent and summed in bfloat16 or wider, within the bound.
A program may use at most 64 MiB of HBM per device.

```python
import jax
import jax.numpy as jnp
from jax import lax

C = 128
CX = 16
CY = 16
NZ = 32


def spiked(drawn, own_key, source, target, blocks, factor):
    owner, partner = [(jnp.arange(drawn.shape[axis_at]) // (drawn.shape[axis_at] // blocks)).reshape([-1 if axis == axis_at else 1 for axis in range(drawn.ndim)]) for axis_at in (source, target)]
    chosen = jax.random.permutation(own_key, blocks)[partner]
    strong = (owner == chosen) | (owner == (partner + blocks // 2) % blocks)
    return jnp.where(strong, factor * drawn, drawn)


def block_scale(key, dims, pieces, smallest, largest):
    def one(axis_at, parts):
        heights = jax.random.uniform(jax.random.fold_in(jax.random.fold_in(key, 6), axis_at), (parts,), jnp.float32, smallest / len(pieces), largest / len(pieces))
        return jnp.repeat(jnp.exp(heights), dims[axis_at] // parts).reshape((-1,) + (1,) * (len(dims) - axis_at - 1))

    loudness = one(*pieces[0])
    for cut in pieces[1:]:
        loudness = loudness * one(*cut)
    return loudness


def bell_draw(stream_key, dims, scale, reach, pieces=(), held_as=jnp.bfloat16):
    gain = block_scale(stream_key, dims, pieces, -0.22, 0.18) if pieces else 1.0
    values = jax.random.normal(stream_key, dims, jnp.float32) * scale * gain
    return jnp.minimum(jnp.maximum(values, -reach), reach).astype(held_as)


def noise_with(own_key, dims, scale, reach, split, heavy, held_as=jnp.bfloat16):
    array = scale * jax.random.normal(own_key, dims, jnp.float32)
    if split:
        array = array * block_scale(own_key, dims, split, -0.22, 0.18)
    return jnp.clip(spiked(array, jax.random.fold_in(own_key, 3), *heavy), -reach, reach).astype(held_as)


def setup_inputs(seed: int = 0, part: int = 0) -> dict:
    splits = jax.random.split(jax.random.key(seed), 5)
    own_keys = jax.random.split(jax.random.fold_in(splits[4], part), 5)
    return {
        "volume": noise_with(own_keys[0], (NZ, CX, CY, C), 1.0, 6.0, ((0, 16),), (0, 3, 16, 2.0)),
        "first_filter": bell_draw(splits[1], (3, 3, 3, C, C), (27 * C) ** -0.5, 0.109375),
        "second_filter": bell_draw(splits[2], (3, 3, 3, C, C), (27 * C) ** -0.5, 0.109375),
        "cotangent": bell_draw(own_keys[3], (NZ, CX, CY, C), (1.0 / (NZ * CX * CY) ** 0.5), 0.06591797, ((0, 16),)),
    }


def spread(field):
    return jnp.pad(field, ((0, 0), (1, 1), (1, 1), (0, 0)))


def convolve(padded, weight):
    depth = padded.shape[0] - 2
    width = padded.shape[1] - 2
    height = padded.shape[2] - 2
    inner = padded.shape[3]
    total = jnp.zeros((depth * width * height, weight.shape[4]), jnp.float32)
    for plane in range(3):
        for column in range(3):
            slab = jnp.concatenate([padded[plane:plane + depth, column:column + width, lane:lane + height, :] for lane in range(3)], axis=-1)
            total = total + jnp.dot(slab.reshape(-1, 3 * inner), weight[plane, column].reshape(3 * inner, -1), preferred_element_type=jnp.float32)
    return total.reshape(depth, width, height, -1)


def weight_term(padded, grads, start, count):
    depth, width, height, outer = grads.shape
    chosen = lax.dynamic_slice_in_dim(padded, start, count, 3)
    flat = grads.reshape(-1, outer)
    blocks = []
    for plane in range(3):
        for column in range(3):
            slab = jnp.concatenate([chosen[plane:plane + depth, column:column + width, lane:lane + height, :] for lane in range(3)], axis=-1)
            term = lax.dot_general(slab.reshape(-1, 3 * count), flat, (((0,), (0,)), ((), ())), preferred_element_type=jnp.float32)
            blocks.append(term.reshape(3, count, outer))
    stacked = jnp.stack(blocks, 0).reshape(3, 3, 3, count, outer)
    return jnp.transpose(stacked, (3, 0, 1, 2, 4))


def flipped(weight):
    return jnp.swapaxes(jnp.flip(weight, (0, 1, 2)), 3, 4)


def reference(volume, first_filter, second_filter, cotangent):
    padded_in = spread(jnp.pad(volume, ((1, 1), (0, 0), (0, 0), (0, 0))))
    hidden = convolve(padded_in, first_filter)
    activated = jax.nn.silu(hidden).astype(jnp.bfloat16)
    padded_act = spread(jnp.pad(activated, ((1, 1), (0, 0), (0, 0), (0, 0))))
    response = convolve(padded_act, second_filter).astype(jnp.bfloat16)
    padded_cot = spread(jnp.pad(cotangent, ((1, 1), (0, 0), (0, 0), (0, 0))))
    act_grad = convolve(padded_cot, flipped(second_filter))
    sigma = jax.nn.sigmoid(hidden)
    hidden_grad = (act_grad * sigma * (1.0 + hidden * (1.0 - sigma))).astype(jnp.bfloat16)
    channels = volume.shape[3]
    second_grad = weight_term(padded_act, cotangent, 0, channels)
    first_grad = weight_term(padded_in, hidden_grad, 0, channels)
    return response, first_grad, second_grad
```

```python
import functools

import jax
import jax.numpy as jnp
from jax import lax
from jax.experimental import pallas as pl
from jax.experimental.pallas import tpu as pltpu
from jax.sharding import PartitionSpec as P

F32, BF16 = jnp.float32, jnp.bfloat16
NT = (((1,), (1,)), ((), ()))


def kernel(
    n, depth, height,
    v_hbm, w1_hbm, w2_hbm, c_hbm,
    resp_ref, g1_ref, g2_ref,
    vb, ab, cg, hg, w1_ref, w2_ref, conv, agr, hid,
    xts, xt, xtc, xvs, xv, xvc, pair, part, b1, r1, bz, rz,
    ins,
    vs, vr, as_, ar, es, er, cs, cr, hs, hr, xs, xr, xes, xer, us, ur, s1, q1, sz, qz,
):
    rows, chans = v_hbm.shape[1:]
    quads = n // 4
    share = chans // n
    class_chans = chans // 4
    planes = 4 * depth
    duo = 2 * depth
    pad = height
    body = pl.ds(pad, rows)
    me = lax.axis_index("space")
    quad = me // 4
    q = lax.rem(me, 4)
    core = lax.rem(q, 2)
    side = q // 2
    mate = quad * 4 + q + 1 - 2 * lax.rem(q, 2)
    twin = quad * 4 + 3 - q
    across = quad * 4 + lax.rem(q + 2, 4)
    first = q * depth
    twin_first = (3 - q) * depth
    mate_first = (q + 1 - 2 * lax.rem(q, 2)) * depth
    across_first = lax.rem(q + 2, 4) * depth

    def remote(src, dst, send, recv, target):
        return pltpu.make_async_remote_copy(
            src_ref=src, dst_ref=dst, send_sem=send, recv_sem=recv,
            device_id={"space": target}, device_id_type=pl.DeviceIdType.MESH,
        )

    load_v = pltpu.make_async_copy(v_hbm, vb.at[pl.ds(1, depth), body], ins.at[0])
    load_c = pltpu.make_async_copy(c_hbm, cg.at[pl.ds(1 + first, depth), body], ins.at[1])
    load_w1 = pltpu.make_async_copy(w1_hbm, w1_ref, ins.at[2])
    load_w2 = pltpu.make_async_copy(w2_hbm, w2_ref, ins.at[3])
    barrier = pltpu.get_barrier_semaphore()
    for d in range(1, n):
        pl.semaphore_signal(
            barrier, inc=1, device_id={"space": lax.rem(me + d, n)},
            device_id_type=pl.DeviceIdType.MESH,
        )
    for copy in (load_v, load_w1, load_c, load_w2):
        copy.start()

    edge = jnp.zeros((pad, chans), BF16)
    for ref in (vb, ab, cg, hg):
        for p in range(ref.shape[0]):
            ref[p, :pad] = edge
            ref[p, pad + rows :] = edge
    plane_of_zeros = jnp.zeros((rows, chans), BF16)
    sliver = jnp.zeros((class_chans, rows), BF16)

    @pl.when(me == 0)
    def _():
        vb[0, body] = plane_of_zeros
        ab[0, body] = plane_of_zeros
        cg[0, body] = plane_of_zeros

    @pl.when(me == n - 1)
    def _():
        vb[depth + 1, body] = plane_of_zeros
        ab[depth + 1, body] = plane_of_zeros
        cg[planes + 1, body] = plane_of_zeros

    @pl.when(quad == 0)
    def _():
        xt[0] = sliver

    @pl.when(quad == quads - 1)
    def _():
        xt[planes + 1] = sliver

    pl.semaphore_wait(barrier, n - 1)

    def rims(low, high, ref, send, recv):
        up = remote(
            high, ref.at[0, body], send.at[0], recv.at[0], lax.rem(me + 1, n)
        )
        down = remote(
            low, ref.at[depth + 1, body], send.at[1], recv.at[1], lax.rem(me + n - 1, n)
        )
        return up, down

    def send_rims(up, down):
        @pl.when(me < n - 1)
        def _():
            up.start()

        @pl.when(me > 0)
        def _():
            down.start()

    def take_rims(up, down):
        @pl.when(me > 0)
        def _():
            up.wait_recv()

        @pl.when(me < n - 1)
        def _():
            down.wait_recv()

    def end_rims(up, down):
        @pl.when(me < n - 1)
        def _():
            up.wait_send()

        @pl.when(me > 0)
        def _():
            down.wait_send()

    v_rims = rims(v_hbm.at[0], v_hbm.at[depth - 1], vb, vs, vr)
    send_rims(*v_rims)

    c_up = remote(c_hbm.at[depth - 1], cg.at[0, body], es.at[0], er.at[0], lax.rem(me + 1, n))
    c_down = remote(
        c_hbm.at[0], cg.at[planes + 1, body], es.at[1], er.at[1], lax.rem(me + n - 1, n)
    )
    sends_up = (q == 3) & (quad < quads - 1)
    sends_down = (q == 0) & (quad > 0)

    @pl.when(sends_up)
    def _():
        c_up.start()

    @pl.when(sends_down)
    def _():
        c_down.start()

    def of_quad(start):
        return cg.at[pl.ds(1 + start, depth), body]

    c_twin = remote(c_hbm, of_quad(first), cs.at[0], cr.at[0], twin)
    c_mate = remote(c_hbm, of_quad(first), cs.at[1], cr.at[1], mate)
    c_onward = remote(of_quad(twin_first), of_quad(twin_first), cs.at[2], cr.at[2], mate)
    c_from_twin = remote(c_hbm, of_quad(twin_first), cs.at[0], cr.at[0], twin)
    c_from_mate = remote(c_hbm, of_quad(mate_first), cs.at[1], cr.at[1], mate)
    c_brought = remote(of_quad(across_first), of_quad(across_first), cs.at[2], cr.at[2], mate)
    c_mate.start()

    slot = lax.broadcasted_iota(jnp.int32, (chans, chans), 0)
    chan = lax.broadcasted_iota(jnp.int32, (chans, chans), 1)
    kind = slot // (2 * class_chans) + 2 * lax.rem(slot // class_chans, 2)
    inner = lax.rem(slot, class_chans)
    wanted = (4 * (inner // share) + kind) * share + lax.rem(inner, share)
    sorter = jnp.where(chan == wanted, 1.0, 0.0).astype(BF16)

    def turn(plane):
        return lax.dot_general(sorter, plane, NT, preferred_element_type=F32).astype(BF16)

    def class_of(device):
        return device - 4 * quad

    def act_slices():
        for p in range(depth):
            turned = turn(ab[1 + p, body])
            for j in range(4):
                top = (j % 2 * 2 + j // 2) * class_chans
                xts[j, p] = turned[top : top + class_chans]
        for i, target in enumerate((twin, across, mate)):
            slice_to(i, target).start()
        for j in range(4):
            up, down = sliver_to(j)

            @pl.when(sends_up)
            def _():
                up.start()

            @pl.when(sends_down)
            def _():
                down.start()

        for p in range(depth):
            xt[1 + first + p] = xts[q, p]

    def slice_to(i, target):
        return remote(
            xts.at[class_of(target)], xt.at[pl.ds(1 + first, depth)],
            xs.at[i], xr.at[i], target,
        )

    def slice_from(i, target):
        return remote(
            xts.at[class_of(target)], xt.at[pl.ds(1 + class_of(target) * depth, depth)],
            xs.at[i], xr.at[i], target,
        )

    def sliver_to(j):
        up = remote(
            xts.at[j, depth - 1], xt.at[0], xes.at[j], xer.at[0],
            lax.rem(quad + 1, quads) * 4 + j,
        )
        down = remote(
            xts.at[j, 0], xt.at[planes + 1], xes.at[j], xer.at[1],
            lax.rem(quad + quads - 1, quads) * 4 + j,
        )
        return up, down

    def take_slices():
        for i, target in enumerate((twin, across, mate)):
            slice_from(i, target).wait_recv()
        up, down = sliver_to(0)

        @pl.when(quad > 0)
        def _():
            up.wait_recv()

        @pl.when(quad < quads - 1)
        def _():
            down.wait_recv()

    def end_slices():
        for i, target in enumerate((twin, across, mate)):
            slice_to(i, target).wait_send()
        for j in range(4):
            up, down = sliver_to(j)

            @pl.when(sends_up)
            def _():
                up.wait_send()

            @pl.when(sends_down)
            def _():
                down.wait_send()

    half = 2 * class_chans
    near = pl.ds(1 + core * depth, depth)
    far = pl.ds(1 + (1 - core) * depth, depth)
    near_rim = core * (duo + 1)
    far_rim = (1 - core) * (duo + 1)

    def vol_turn(p, plane):
        turned = turn(plane)
        for j in range(2):
            xvs[j, p] = turned[j * half : (j + 1) * half]

    v_mate = remote(xvs.at[1 - core, pl.ds(0, depth)], xv.at[near], us.at[0], ur.at[0], mate)
    v_from_mate = remote(xvs.at[1 - core, pl.ds(0, depth)], xv.at[far], us.at[0], ur.at[0], mate)
    v_rim_mate = remote(xvs.at[1 - core, depth], xv.at[near_rim], us.at[1], ur.at[1], mate)
    v_rim_from_mate = remote(xvs.at[1 - core, depth], xv.at[far_rim], us.at[1], ur.at[1], mate)

    h_near = hg.at[pl.ds(core * depth, depth), body]
    h_far = hg.at[pl.ds((1 - core) * depth, depth), body]
    h_mate = remote(h_near, h_near, hs.at[0], hr.at[0], mate)
    h_from_mate = remote(h_near, h_far, hs.at[0], hr.at[0], mate)

    def wide(ref, plane):
        return jnp.concatenate(
            [ref[plane, b * pad : b * pad + rows] for b in range(3)], axis=1
        )

    def w_first(a):
        return jnp.concatenate(
            [
                jnp.concatenate([w1_ref[a * 9 + b * 3 + c] for b in range(3)], axis=0)
                for c in range(3)
            ],
            axis=1,
        )

    def w_second(a):
        return jnp.concatenate(
            [
                jnp.concatenate([w2_ref[a * 9 + b * 3 + c] for b in range(3)], axis=0)
                for c in range(3)
            ],
            axis=1,
        )

    def w_turned(a):
        return jnp.concatenate(
            [
                jnp.concatenate([w2_ref[26 - (a * 9 + b * 3 + c)] for b in range(3)], axis=1)
                for c in range(3)
            ],
            axis=0,
        )

    def mul(x, w):
        return jnp.dot(x, w, preferred_element_type=F32)

    def mul_turned(x, w):
        return lax.dot_general(x, w, NT, preferred_element_type=F32)

    lane = lax.rem(lax.broadcasted_iota(jnp.int32, (rows, chans), 0), height)

    def fold(y):
        before = jnp.where(lane == 0, 0.0, pltpu.roll(y[:, :chans], 1, 0))
        after = jnp.where(lane == height - 1, 0.0, pltpu.roll(y[:, 2 * chans :], rows - 1, 0))
        return before + y[:, chans : 2 * chans] + after

    def inner_part(ref, base, w, product, acc):
        for p in range(depth):
            total = None
            for r in range(depth):
                a = r - p + 1
                if 0 <= a <= 2:
                    term = product(wide(ref, base + 1 + r), w(a))
                    total = term if total is None else total + term
            acc[p] = total

    def outer_part(ref, base, w, product, acc):
        low = acc[0] + product(wide(ref, base), w(0))
        if depth == 1:
            return (low + product(wide(ref, base + 2), w(2)),)
        mids = tuple(acc[p] for p in range(1, depth - 1))
        high = acc[depth - 1] + product(wide(ref, base + depth + 1), w(2))
        return (low,) + mids + (high,)

    load_v.wait()
    for p in range(depth):
        vol_turn(p, vb[1 + p, body])
        xv[1 + core * depth + p] = xvs[core, p]
    v_mate.start()
    load_w1.wait()
    inner_part(vb, 0, w_first, mul, conv)
    c_twin.start()
    load_c.wait()
    load_w2.wait()
    inner_part(cg, first, w_turned, mul_turned, agr)

    take_rims(*v_rims)
    for p, y in enumerate(outer_part(vb, 0, w_first, mul, conv)):
        h = fold(y)
        hid[p] = h
        ab[1 + p, body] = (h * jax.nn.sigmoid(h)).astype(BF16)
    act_slices()

    vol_turn(depth, vb[core * (depth + 1), body])
    xv[near_rim] = xvs[core, depth]
    v_rim_mate.start()

    c_from_twin.wait_recv()
    c_onward.start()
    c_from_mate.wait_recv()

    @pl.when((q == 0) & (quad > 0))
    def _():
        c_up.wait_recv()

    @pl.when((q == 3) & (quad < quads - 1))
    def _():
        c_down.wait_recv()

    for p, y in enumerate(outer_part(cg, first, w_turned, mul_turned, agr)):
        h = hid[p]
        s = jax.nn.sigmoid(h)
        hg[core * depth + p, body] = (fold(y) * s * (1.0 + h * (1.0 - s))).astype(BF16)
    h_mate.start()

    step = lax.rem(lax.broadcasted_iota(jnp.int32, (class_chans, rows), 1), height)

    def shift_slices(src, dst, count, tall):
        for s in range(count):
            for i in range(tall // class_chans):
                cols = slice(s * rows, (s + 1) * rows)
                x = src[s, i * class_chans : (i + 1) * class_chans]
                w = x.astype(F32)
                before = jnp.where(step == 0, 0.0, pltpu.roll(w, 1, 1)).astype(BF16)
                after = jnp.where(step == height - 1, 0.0, pltpu.roll(w, rows - 1, 1)).astype(BF16)
                for c, moved in enumerate((before, x, after)):
                    top = c * tall + i * class_chans
                    dst[top : top + class_chans, cols] = moved

    def product_of(xs_ref, a, field, lead, count):
        taps = jnp.concatenate(
            [
                jnp.concatenate(
                    [field[lead + p, (2 - b) * pad : (2 - b) * pad + rows] for b in range(3)],
                    axis=1,
                )
                for p in range(count)
            ],
            axis=0,
        )
        return mul(xs_ref[:, a * rows : (a + count) * rows], taps)

    def across_hop(k):
        return remote(b1.at[k], r1.at[k], s1.at[k], q1.at[k], across)

    def first_piece(a):
        term = product_of(xvc, a, hg, 0, duo)
        for i in range(2):
            for z in range(quads):
                for b in range(3):
                    for c in range(3):
                        top = c * half + i * class_chans + z * share
                        pair[a, i, z, 3 * b + c] = term[
                            top : top + share, b * chans : (b + 1) * chans
                        ]
        b1[a] = pair[a, 1 - side].astype(BF16)
        across_hop(a).start()

    def second_piece(a):
        term = product_of(xtc, a, cg, 1, planes)
        for z in range(quads):
            for b in range(3):
                for c in range(3):
                    top = c * class_chans + z * share
                    part[3 + a, z, 3 * b + c] = term[
                        top : top + share, b * chans : (b + 1) * chans
                    ]
        z_send(3 + a, 0)

    def first_arrives(a):
        across_hop(a).wait_recv()
        part[a] = pair[a, side] + r1[a].astype(F32)
        z_send(a, 0)

    levels = quads.bit_length() - 1
    starts = [sum(quads >> (m + 1) for m in range(level)) for level in range(levels)]

    def bit(level):
        return lax.rem(quad // (1 << level), 2)

    def partner(level):
        return quad + (1 - 2 * bit(level)) * (1 << level)

    def z_hop(k, level):
        block = pl.ds(starts[level], quads >> (level + 1))
        return remote(
            bz.at[k, block], rz.at[k, block], sz.at[k, level], qz.at[k, level],
            partner(level) * 4 + q,
        )

    def z_send(k, level):
        for i in range(quads >> (level + 1)):
            bz[k, starts[level] + i] = part[k, 2 * i + 1 - bit(level)].astype(BF16)
        z_hop(k, level).start()

    def z_take(k, level):
        z_hop(k, level).wait_recv()
        for i in range(quads >> (level + 1)):
            total = part[k, 2 * i + bit(level)] + rz[k, starts[level] + i].astype(F32)
            if level < levels - 1:
                part[k, i] = total
            else:
                (g1_ref, g2_ref)[k // 3][9 * (k % 3) : 9 * (k % 3) + 9] = total
        if level < levels - 1:
            z_send(k, level + 1)

    v_from_mate.wait_recv()
    v_rim_from_mate.wait_recv()
    shift_slices(xv, xvc, duo + 2, half)
    h_from_mate.wait_recv()
    for a in range(3):
        first_piece(a)
    act_rims = rims(ab.at[1, body], ab.at[depth, body], ab, as_, ar)
    send_rims(*act_rims)

    take_slices()
    shift_slices(xt, xtc, planes + 2, class_chans)
    c_brought.wait_recv()
    for a in range(3):
        second_piece(a)
    inner_part(ab, 0, w_second, mul, conv)
    first_arrives(0)
    z_take(3, 0)
    first_arrives(1)
    z_take(4, 0)
    first_arrives(2)
    z_take(5, 0)

    take_rims(*act_rims)
    for p, y in enumerate(outer_part(ab, 0, w_second, mul, conv)):
        resp_ref[p] = fold(y).astype(BF16)
    for k in range(3):
        z_take(k, 0)
    for level in range(1, levels):
        for k in (3, 4, 5, 0, 1, 2):
            z_take(k, level)

    end_rims(*v_rims)
    end_rims(*act_rims)

    @pl.when(sends_up)
    def _():
        c_up.wait_send()

    @pl.when(sends_down)
    def _():
        c_down.wait_send()

    for copy in (c_twin, c_mate, c_onward, v_mate, v_rim_mate, h_mate):
        copy.wait_send()
    end_slices()
    for a in range(3):
        across_hop(a).wait_send()
    for k in range(6):
        for level in range(levels):
            z_hop(k, level).wait_send()


def put(resp, g1, g2, resp_hbm, g1_hbm, g2_hbm, sems):
    pairs = ((resp, resp_hbm), (g1, g1_hbm), (g2, g2_hbm))
    copies = [pltpu.make_async_copy(src, dst, sems.at[i]) for i, (src, dst) in enumerate(pairs)]
    for copy in copies:
        copy.start()
    for copy in copies:
        copy.wait()


def per_device(n, volume, first_filter, second_filter, cotangent):
    depth, width, height, chans = volume.shape
    rows = width * height
    share = chans // n
    quads = n // 4
    planes = 4 * depth
    tall = rows + 2 * height
    class_chans = chans // 4
    levels = quads.bit_length() - 1
    dma = pltpu.SemaphoreType.DMA
    hbm = pl.BlockSpec(memory_space=pl.ANY)
    block = (27, share, chans)
    piece = (9, share, chans)
    vmem = pltpu.VMEM
    response, first, second = pl.pallas_call(
        functools.partial(kernel, n, depth, height),
        out_shape=(
            pltpu.VMEM((depth, rows, chans), BF16),
            pltpu.VMEM(block, F32),
            pltpu.VMEM(block, F32),
        ),
        in_specs=[hbm] * 4,
        out_specs=(pl.BlockSpec(memory_space=pltpu.VMEM),) * 3,
        scratch_shapes=[
            vmem((depth + 2, tall, chans), BF16),
            vmem((depth + 2, tall, chans), BF16),
            vmem((planes + 2, tall, chans), BF16),
            vmem((2 * depth, tall, chans), BF16),
            vmem((27, chans, chans), BF16),
            vmem((27, chans, chans), BF16),
            vmem((depth, rows, 3 * chans), F32),
            vmem((depth, rows, 3 * chans), F32),
            vmem((depth, rows, chans), F32),
            vmem((4, depth, class_chans, rows), BF16),
            vmem((planes + 2, class_chans, rows), BF16),
            vmem((3 * class_chans, (planes + 2) * rows), BF16),
            vmem((2, depth + 1, 2 * class_chans, rows), BF16),
            vmem((2 * depth + 2, 2 * class_chans, rows), BF16),
            vmem((6 * class_chans, (2 * depth + 2) * rows), BF16),
            vmem((3, 2, quads) + piece, F32),
            vmem((6, quads) + piece, F32),
            vmem((3, quads) + piece, BF16),
            vmem((3, quads) + piece, BF16),
            vmem((6, quads) + piece, BF16),
            vmem((6, quads) + piece, BF16),
            dma((4,)),
            dma((2,)), dma((2,)), dma((2,)), dma((2,)), dma((2,)), dma((2,)),
            dma((3,)), dma((3,)), dma((1,)), dma((1,)),
            dma((3,)), dma((3,)), dma((4,)), dma((2,)), dma((2,)), dma((2,)),
            dma((3,)), dma((3,)), dma((6, levels)), dma((6, levels)),
        ],
        compiler_params=pltpu.CompilerParams(
            collective_id=0, has_side_effects=True, vmem_limit_bytes=58 * 1024 * 1024
        ),
    )(
        volume.reshape(depth, rows, chans),
        first_filter.reshape(27, chans, chans),
        second_filter.reshape(27, chans, chans),
        cotangent.reshape(depth, rows, chans),
    )
    response, first, second = pl.pallas_call(
        put,
        out_shape=(
            jax.ShapeDtypeStruct((depth, rows, chans), BF16),
            jax.ShapeDtypeStruct(block, F32),
            jax.ShapeDtypeStruct(block, F32),
        ),
        in_specs=[pl.BlockSpec(memory_space=pltpu.VMEM)] * 3,
        out_specs=(hbm,) * 3,
        scratch_shapes=[dma((3,))],
    )(*(pltpu.with_memory_space_constraint(x, pltpu.VMEM) for x in (response, first, second)))

    def laid(grad):
        return jnp.transpose(grad, (1, 0, 2)).reshape(share, 3, 3, 3, chans)

    return response.reshape(volume.shape), laid(first), laid(second)


def solution(mesh):
    n = mesh.shape["space"]
    field = P(("parts", "space"), None, None, None)
    grad = P(("parts", "space"), None, None, None, None)
    return jax.shard_map(
        functools.partial(per_device, n),
        mesh=mesh,
        in_specs=(field, P(), P(), field),
        out_specs=(field, grad, grad),
        check_vma=False,
    )
```

```python
import functools

import jax
import jax.numpy as jnp
from jax import lax
from jax.experimental import pallas as pl
from jax.experimental.pallas import tpu as pltpu
from jax.sharding import PartitionSpec as P

F32, BF16 = jnp.float32, jnp.bfloat16
NT = (((1,), (1,)), ((), ()))
ORDERS = [[0, 1, 'y'], ['y', 0, 1], ['y', 0, 1], [0, 1], [0, 1], [0, 1]]
TAKES = ([(0, 0), (1, 0), (2, 0), (3, 0), (4, 0), (5, 0)], [(0, 1), (1, 1), (2, 1), (3, 1), (4, 1), (5, 1), (0, 2), (1, 2), (2, 2)])


def kernel(
    n, depth, height,
    v_hbm, w1_hbm, w2_hbm, c_hbm,
    resp_ref, g1_ref, g2_ref,
    vb, ab, cg, hg, w1_ref, w2_ref, conv, agr, hid,
    xts, xt, xtc, xvs, xv, xvc, part, bz, rz,
    ins,
    vs, vr, as_, ar, es, er, ts, tr, cs, cr, hs, hr, xs, xr, xes, xer, us, ur, sz, qz,
):
    rows, chans = v_hbm.shape[1:]
    quads = n // 4
    share = chans // n
    class_chans = chans // 4
    planes = 4 * depth
    duo = 2 * depth
    pad = height
    body = pl.ds(pad, rows)
    me = lax.axis_index("space")
    quad = me // 4
    q = lax.rem(me, 4)
    core = lax.rem(q, 2)
    side = q // 2
    mate = quad * 4 + q + 1 - 2 * lax.rem(q, 2)
    twin = quad * 4 + 3 - q
    across = quad * 4 + lax.rem(q + 2, 4)
    first = q * depth
    twin_first = (3 - q) * depth
    mate_first = (q + 1 - 2 * lax.rem(q, 2)) * depth
    across_first = lax.rem(q + 2, 4) * depth

    def remote(src, dst, send, recv, target):
        return pltpu.make_async_remote_copy(
            src_ref=src, dst_ref=dst, send_sem=send, recv_sem=recv,
            device_id={"space": target}, device_id_type=pl.DeviceIdType.MESH,
        )

    load_v = pltpu.make_async_copy(v_hbm, vb.at[pl.ds(1, depth), body], ins.at[0])
    load_c = pltpu.make_async_copy(c_hbm, cg.at[pl.ds(1 + first, depth), body], ins.at[1])
    load_w1 = pltpu.make_async_copy(w1_hbm, w1_ref, ins.at[2])
    load_w2 = pltpu.make_async_copy(w2_hbm, w2_ref, ins.at[3])
    barrier = pltpu.get_barrier_semaphore()
    for d in range(1, n):
        pl.semaphore_signal(
            barrier, inc=1, device_id={"space": lax.rem(me + d, n)},
            device_id_type=pl.DeviceIdType.MESH,
        )
    for copy in (load_v, load_w1, load_c, load_w2):
        copy.start()

    edge = jnp.zeros((pad, chans), BF16)
    for ref in (vb, ab, cg, hg):
        for p in range(ref.shape[0]):
            ref[p, :pad] = edge
            ref[p, pad + rows :] = edge
    plane_of_zeros = jnp.zeros((rows, chans), BF16)
    sliver = jnp.zeros((class_chans, rows), BF16)

    @pl.when(me == 0)
    def _():
        vb[0, body] = plane_of_zeros
        ab[0, body] = plane_of_zeros
        cg[0, body] = plane_of_zeros

    @pl.when(me == n - 1)
    def _():
        vb[depth + 1, body] = plane_of_zeros
        ab[depth + 1, body] = plane_of_zeros
        cg[planes + 1, body] = plane_of_zeros

    @pl.when(quad == 0)
    def _():
        xt[0] = sliver

    @pl.when(quad == quads - 1)
    def _():
        xt[planes + 1] = sliver

    pl.semaphore_wait(barrier, n - 1)

    def rims(low, high, ref, send, recv):
        up = remote(
            high, ref.at[0, body], send.at[0], recv.at[0], lax.rem(me + 1, n)
        )
        down = remote(
            low, ref.at[depth + 1, body], send.at[1], recv.at[1], lax.rem(me + n - 1, n)
        )
        return up, down

    def send_rims(up, down):
        @pl.when(me < n - 1)
        def _():
            up.start()

        @pl.when(me > 0)
        def _():
            down.start()

    def take_rims(up, down):
        @pl.when(me > 0)
        def _():
            up.wait_recv()

        @pl.when(me < n - 1)
        def _():
            down.wait_recv()

    def end_rims(up, down):
        @pl.when(me < n - 1)
        def _():
            up.wait_send()

        @pl.when(me > 0)
        def _():
            down.wait_send()

    v_rims = rims(v_hbm.at[0], v_hbm.at[depth - 1], vb, vs, vr)
    send_rims(*v_rims)

    c_up = remote(c_hbm.at[depth - 1], cg.at[0, body], es.at[0], er.at[0], lax.rem(me + 1, n))
    c_down = remote(
        c_hbm.at[0], cg.at[planes + 1, body], es.at[1], er.at[1], lax.rem(me + n - 1, n)
    )
    sends_up = (q == 3) & (quad < quads - 1)
    sends_down = (q == 0) & (quad > 0)

    @pl.when(sends_up)
    def _():
        c_up.start()

    @pl.when(sends_down)
    def _():
        c_down.start()

    def of_quad(start):
        return cg.at[pl.ds(1 + start, depth), body]

    def twin_plane(i):
        out = abs_order(side, i)
        back = abs_order(1 - side, i)
        there = cg.at[1 + first + out, body]
        here = cg.at[1 + twin_first + back, body]
        to = remote(c_hbm.at[out], there, ts.at[i], tr.at[i], twin)
        back_from = remote(c_hbm.at[out], here, ts.at[i], tr.at[i], twin)
        return to, back_from

    def abs_order(at_side, i):
        return (1 - at_side) * (depth - 1 - i) + at_side * i

    twin_planes = [twin_plane(i) for i in range(depth)]
    c_mate = remote(c_hbm, of_quad(first), cs.at[1], cr.at[1], mate)
    c_onward = remote(of_quad(twin_first), of_quad(twin_first), cs.at[2], cr.at[2], mate)
    c_from_mate = remote(c_hbm, of_quad(mate_first), cs.at[1], cr.at[1], mate)
    c_brought = remote(of_quad(across_first), of_quad(across_first), cs.at[2], cr.at[2], mate)
    beside_twin = (q == 1) | (q == 2)

    @pl.when(beside_twin)
    def _():
        twin_planes[0][0].start()

    c_mate.start()

    slot = lax.broadcasted_iota(jnp.int32, (chans, chans), 0)
    chan = lax.broadcasted_iota(jnp.int32, (chans, chans), 1)
    kind = slot // (2 * class_chans) + 2 * lax.rem(slot // class_chans, 2)
    inner = lax.rem(slot, class_chans)
    wanted = (4 * (inner // share) + kind) * share + lax.rem(inner, share)
    sorter = jnp.where(chan == wanted, 1.0, 0.0).astype(BF16)

    def turn(plane):
        return lax.dot_general(sorter, plane, NT, preferred_element_type=F32).astype(BF16)

    def class_of(device):
        return device - 4 * quad

    def act_slices():
        for p in range(depth):
            turned = turn(ab[1 + p, body])
            for j in range(4):
                top = (j % 2 * 2 + j // 2) * class_chans
                xts[j, p] = turned[top : top + class_chans]
        for i, target in enumerate((twin, across, mate)):
            slice_to(i, target).start()
        for j in range(4):
            up, down = sliver_to(j)

            @pl.when(sends_up)
            def _():
                up.start()

            @pl.when(sends_down)
            def _():
                down.start()

        for p in range(depth):
            xt[1 + first + p] = xts[q, p]

    def slice_to(i, target):
        return remote(
            xts.at[class_of(target)], xt.at[pl.ds(1 + first, depth)],
            xs.at[i], xr.at[i], target,
        )

    def slice_from(i, target):
        return remote(
            xts.at[class_of(target)], xt.at[pl.ds(1 + class_of(target) * depth, depth)],
            xs.at[i], xr.at[i], target,
        )

    def sliver_to(j):
        up = remote(
            xts.at[j, depth - 1], xt.at[0], xes.at[j], xer.at[0],
            lax.rem(quad + 1, quads) * 4 + j,
        )
        down = remote(
            xts.at[j, 0], xt.at[planes + 1], xes.at[j], xer.at[1],
            lax.rem(quad + quads - 1, quads) * 4 + j,
        )
        return up, down

    def take_slices():
        for i, target in enumerate((twin, across, mate)):
            slice_from(i, target).wait_recv()
        up, down = sliver_to(0)

        @pl.when(quad > 0)
        def _():
            up.wait_recv()

        @pl.when(quad < quads - 1)
        def _():
            down.wait_recv()

    def end_slices():
        for i, target in enumerate((twin, across, mate)):
            slice_to(i, target).wait_send()
        for j in range(4):
            up, down = sliver_to(j)

            @pl.when(sends_up)
            def _():
                up.wait_send()

            @pl.when(sends_down)
            def _():
                down.wait_send()

    half = 2 * class_chans
    near = pl.ds(1 + core * depth, depth)
    far = pl.ds(1 + (1 - core) * depth, depth)
    near_rim = core * (duo + 1)
    far_rim = (1 - core) * (duo + 1)

    def vol_turn(p, plane):
        turned = turn(plane)
        for j in range(2):
            xvs[j, p] = turned[j * half : (j + 1) * half]

    v_mate = remote(xvs.at[1 - core, pl.ds(0, depth)], xv.at[near], us.at[0], ur.at[0], mate)
    v_from_mate = remote(xvs.at[1 - core, pl.ds(0, depth)], xv.at[far], us.at[0], ur.at[0], mate)
    v_rim_mate = remote(xvs.at[1 - core, depth], xv.at[near_rim], us.at[1], ur.at[1], mate)
    v_rim_from_mate = remote(xvs.at[1 - core, depth], xv.at[far_rim], us.at[1], ur.at[1], mate)

    h_near = hg.at[pl.ds(core * depth, depth), body]
    h_far = hg.at[pl.ds((1 - core) * depth, depth), body]
    h_mate = remote(h_near, h_near, hs.at[0], hr.at[0], mate)
    h_from_mate = remote(h_near, h_far, hs.at[0], hr.at[0], mate)

    def wide(ref, plane):
        return jnp.concatenate(
            [ref[plane, b * pad : b * pad + rows] for b in range(3)], axis=1
        )

    def w_first(a):
        return jnp.concatenate(
            [
                jnp.concatenate([w1_ref[a * 9 + b * 3 + c] for b in range(3)], axis=0)
                for c in range(3)
            ],
            axis=1,
        )

    def w_second(a):
        return jnp.concatenate(
            [
                jnp.concatenate([w2_ref[a * 9 + b * 3 + c] for b in range(3)], axis=0)
                for c in range(3)
            ],
            axis=1,
        )

    def w_turned(a):
        return jnp.concatenate(
            [
                jnp.concatenate([w2_ref[26 - (a * 9 + b * 3 + c)] for b in range(3)], axis=1)
                for c in range(3)
            ],
            axis=0,
        )

    def mul(x, w):
        return jnp.dot(x, w, preferred_element_type=F32)

    def mul_turned(x, w):
        return lax.dot_general(x, w, NT, preferred_element_type=F32)

    lane = lax.rem(lax.broadcasted_iota(jnp.int32, (rows, chans), 0), height)

    def fold(y):
        before = jnp.where(lane == 0, 0.0, pltpu.roll(y[:, :chans], 1, 0))
        after = jnp.where(lane == height - 1, 0.0, pltpu.roll(y[:, 2 * chans :], rows - 1, 0))
        return before + y[:, chans : 2 * chans] + after

    def inner_part(ref, base, w, product, acc):
        for p in range(depth):
            total = None
            for r in range(depth):
                a = r - p + 1
                if 0 <= a <= 2:
                    term = product(wide(ref, base + 1 + r), w(a))
                    total = term if total is None else total + term
            acc[p] = total

    def outer_part(ref, base, w, product, acc):
        low = acc[0] + product(wide(ref, base), w(0))
        if depth == 1:
            return (low + product(wide(ref, base + 2), w(2)),)
        mids = tuple(acc[p] for p in range(1, depth - 1))
        high = acc[depth - 1] + product(wide(ref, base + depth + 1), w(2))
        return (low,) + mids + (high,)

    load_v.wait()
    for p in range(depth):
        vol_turn(p, vb[1 + p, body])
        xv[1 + core * depth + p] = xvs[core, p]
    v_mate.start()
    load_w1.wait()
    inner_part(vb, 0, w_first, mul, conv)
    @pl.when(jnp.logical_not(beside_twin))
    def _():
        twin_planes[0][0].start()

    for to, _ in twin_planes[1:]:
        to.start()
    load_c.wait()
    load_w2.wait()
    inner_part(cg, first, w_turned, mul_turned, agr)

    take_rims(*v_rims)
    for p, y in enumerate(outer_part(vb, 0, w_first, mul, conv)):
        h = fold(y)
        hid[p] = h
        ab[1 + p, body] = (h * jax.nn.sigmoid(h)).astype(BF16)
    act_slices()

    vol_turn(depth, vb[core * (depth + 1), body])
    xv[near_rim] = xvs[core, depth]
    v_rim_mate.start()

    @pl.when(beside_twin)
    def _():
        twin_planes[0][1].wait_recv()

    c_from_mate.wait_recv()

    @pl.when((q == 0) & (quad > 0))
    def _():
        c_up.wait_recv()

    @pl.when((q == 3) & (quad < quads - 1))
    def _():
        c_down.wait_recv()

    for p, y in enumerate(outer_part(cg, first, w_turned, mul_turned, agr)):
        h = hid[p]
        s = jax.nn.sigmoid(h)
        hg[core * depth + p, body] = (fold(y) * s * (1.0 + h * (1.0 - s))).astype(BF16)
    h_mate.start()

    step = lax.rem(lax.broadcasted_iota(jnp.int32, (class_chans, rows), 1), height)

    def shift_slices(src, dst, count, tall):
        for s in range(count):
            for i in range(tall // class_chans):
                cols = slice(s * rows, (s + 1) * rows)
                x = src[s, i * class_chans : (i + 1) * class_chans]
                w = x.astype(F32)
                before = jnp.where(step == 0, 0.0, pltpu.roll(w, 1, 1)).astype(BF16)
                after = jnp.where(step == height - 1, 0.0, pltpu.roll(w, rows - 1, 1)).astype(BF16)
                for c, moved in enumerate((before, x, after)):
                    top = c * tall + i * class_chans
                    dst[top : top + class_chans, cols] = moved

    def product_of(xs_ref, a, field, lead, count):
        taps = jnp.concatenate(
            [
                jnp.concatenate(
                    [field[lead + p, (2 - b) * pad : (2 - b) * pad + rows] for b in range(3)],
                    axis=1,
                )
                for p in range(count)
            ],
            axis=0,
        )
        return mul(xs_ref[:, a * rows : (a + count) * rows], taps)

    def bit(axis):
        return side if axis == "y" else lax.rem(quad // (1 << axis), 2)

    def partner(axis):
        if axis == "y":
            return across
        return (quad + (1 - 2 * bit(axis)) * (1 << axis)) * 4 + q

    levels = quads.bit_length() - 1
    axes = list(range(levels))[::-1]

    def plan(k):
        order = ORDERS[k] + [axis for axis in range(2, levels)]
        left = (["y"] if k < 3 else []) + axes
        steps, start = [], 0
        for axis in order:
            count = 1 << (len(left) - 1)
            stride = 1 << (len(left) - 1 - left.index(axis))
            steps.append((axis, count, stride, start))
            left.remove(axis)
            start += count
        return steps

    plans = [plan(k) for k in range(6)]

    def place(i, stride, which):
        return i // stride * 2 * stride + which * stride + i % stride

    def hop(k, level):
        axis, count, stride, start = plans[k][level]
        return remote(
            bz.at[k, pl.ds(start, count)], rz.at[k, pl.ds(start, count)],
            sz.at[k, level], qz.at[k, level], partner(axis),
        )

    def give(k, level):
        axis, count, stride, start = plans[k][level]
        for i in range(count):
            bz[k, start + i] = part[k, place(i, stride, 1 - bit(axis))].astype(BF16)
        hop(k, level).start()

    def take(k, level):
        axis, count, stride, start = plans[k][level]
        hop(k, level).wait_recv()
        for i in range(count):
            total = part[k, place(i, stride, bit(axis))] + rz[k, start + i].astype(F32)
            if level + 1 < len(plans[k]):
                part[k, i] = total
            else:
                (g1_ref, g2_ref)[k // 3][9 * (k % 3) : 9 * (k % 3) + 9] = total
        if level + 1 < len(plans[k]):
            give(k, level + 1)

    def first_piece(a):
        term = product_of(xvc, a, hg, 0, duo)
        for i in range(2):
            for z in range(quads):
                for b in range(3):
                    for c in range(3):
                        top = c * half + i * class_chans + z * share
                        part[a, i * quads + z, 3 * b + c] = term[
                            top : top + share, b * chans : (b + 1) * chans
                        ]
        give(a, 0)

    def second_piece(a):
        term = product_of(xtc, a, cg, 1, planes)
        for z in range(quads):
            for b in range(3):
                for c in range(3):
                    top = c * class_chans + z * share
                    part[3 + a, z, 3 * b + c] = term[
                        top : top + share, b * chans : (b + 1) * chans
                    ]
        give(3 + a, 0)

    v_from_mate.wait_recv()
    v_rim_from_mate.wait_recv()
    shift_slices(xv, xvc, duo + 2, half)
    h_from_mate.wait_recv()
    for a in range(3):
        first_piece(a)

    @pl.when(jnp.logical_not(beside_twin))
    def _():
        twin_planes[0][1].wait_recv()

    for _, back in twin_planes[1:]:
        back.wait_recv()
    c_onward.start()
    act_rims = rims(ab.at[1, body], ab.at[depth, body], ab, as_, ar)
    send_rims(*act_rims)

    take_slices()
    shift_slices(xt, xtc, planes + 2, class_chans)
    c_brought.wait_recv()
    for a in range(3):
        second_piece(a)
    inner_part(ab, 0, w_second, mul, conv)
    for k, level in TAKES[0]:
        take(k, level)
    take_rims(*act_rims)
    for p, y in enumerate(outer_part(ab, 0, w_second, mul, conv)):
        resp_ref[p] = fold(y).astype(BF16)
    for k, level in TAKES[1]:
        take(k, level)
    for level in range(2, len(plans[0])):
        for k in range(6):
            if (k, level) not in TAKES[1] and level < len(plans[k]):
                take(k, level)

    end_rims(*v_rims)
    end_rims(*act_rims)

    @pl.when(sends_up)
    def _():
        c_up.wait_send()

    @pl.when(sends_down)
    def _():
        c_down.wait_send()

    for to, _ in twin_planes:
        to.wait_send()
    for copy in (c_mate, c_onward, v_mate, v_rim_mate, h_mate):
        copy.wait_send()
    end_slices()
    for k in range(6):
        for level in range(len(plans[k])):
            hop(k, level).wait_send()


def put(resp, g1, g2, resp_hbm, g1_hbm, g2_hbm, sems):
    pairs = ((resp, resp_hbm), (g1, g1_hbm), (g2, g2_hbm))
    copies = [pltpu.make_async_copy(src, dst, sems.at[i]) for i, (src, dst) in enumerate(pairs)]
    for copy in copies:
        copy.start()
    for copy in copies:
        copy.wait()


def per_device(n, volume, first_filter, second_filter, cotangent):
    depth, width, height, chans = volume.shape
    rows = width * height
    share = chans // n
    quads = n // 4
    planes = 4 * depth
    tall = rows + 2 * height
    class_chans = chans // 4
    levels = quads.bit_length() - 1
    dma = pltpu.SemaphoreType.DMA
    hbm = pl.BlockSpec(memory_space=pl.ANY)
    block = (27, share, chans)
    piece = (9, share, chans)
    vmem = pltpu.VMEM
    response, first, second = pl.pallas_call(
        functools.partial(kernel, n, depth, height),
        out_shape=(
            pltpu.VMEM((depth, rows, chans), BF16),
            pltpu.VMEM(block, F32),
            pltpu.VMEM(block, F32),
        ),
        in_specs=[hbm] * 4,
        out_specs=(pl.BlockSpec(memory_space=pltpu.VMEM),) * 3,
        scratch_shapes=[
            vmem((depth + 2, tall, chans), BF16),
            vmem((depth + 2, tall, chans), BF16),
            vmem((planes + 2, tall, chans), BF16),
            vmem((2 * depth, tall, chans), BF16),
            vmem((27, chans, chans), BF16),
            vmem((27, chans, chans), BF16),
            vmem((depth, rows, 3 * chans), F32),
            vmem((depth, rows, 3 * chans), F32),
            vmem((depth, rows, chans), F32),
            vmem((4, depth, class_chans, rows), BF16),
            vmem((planes + 2, class_chans, rows), BF16),
            vmem((3 * class_chans, (planes + 2) * rows), BF16),
            vmem((2, depth + 1, 2 * class_chans, rows), BF16),
            vmem((2 * depth + 2, 2 * class_chans, rows), BF16),
            vmem((6 * class_chans, (2 * depth + 2) * rows), BF16),
            vmem((6, 2 * quads) + piece, F32),
            vmem((6, 2 * quads) + piece, BF16),
            vmem((6, 2 * quads) + piece, BF16),
            dma((4,)),
            dma((2,)), dma((2,)), dma((2,)), dma((2,)), dma((2,)), dma((2,)),
            dma((depth,)), dma((depth,)), dma((3,)), dma((3,)), dma((1,)), dma((1,)),
            dma((3,)), dma((3,)), dma((4,)), dma((2,)), dma((2,)), dma((2,)),
            dma((6, levels + 1)), dma((6, levels + 1)),
        ],
        compiler_params=pltpu.CompilerParams(
            collective_id=0, has_side_effects=True, vmem_limit_bytes=58 * 1024 * 1024
        ),
    )(
        volume.reshape(depth, rows, chans),
        first_filter.reshape(27, chans, chans),
        second_filter.reshape(27, chans, chans),
        cotangent.reshape(depth, rows, chans),
    )
    response, first, second = pl.pallas_call(
        put,
        out_shape=(
            jax.ShapeDtypeStruct((depth, rows, chans), BF16),
            jax.ShapeDtypeStruct(block, F32),
            jax.ShapeDtypeStruct(block, F32),
        ),
        in_specs=[pl.BlockSpec(memory_space=pltpu.VMEM)] * 3,
        out_specs=(hbm,) * 3,
        scratch_shapes=[dma((3,))],
    )(*(pltpu.with_memory_space_constraint(x, pltpu.VMEM) for x in (response, first, second)))

    def laid(grad):
        return jnp.transpose(grad, (1, 0, 2)).reshape(share, 3, 3, 3, chans)

    return response.reshape(volume.shape), laid(first), laid(second)


def solution(mesh):
    n = mesh.shape["space"]
    field = P(("parts", "space"), None, None, None)
    grad = P(("parts", "space"), None, None, None, None)
    return jax.shard_map(
        functools.partial(per_device, n),
        mesh=mesh,
        in_specs=(field, P(), P(), field),
        out_specs=(field, grad, grad),
        check_vma=False,
    )
```

```python
import functools

import jax
import jax.numpy as jnp
from jax import lax
from jax.experimental import pallas as pl
from jax.experimental.pallas import tpu as pltpu
from jax.sharding import PartitionSpec as P

F32, BF16 = jnp.float32, jnp.bfloat16
NT = (((1,), (1,)), ((), ()))
ORDERS = [[0, 1, 'y'], ['y', 0, 1], ['y', 0, 1], [0, 1], [0, 1], [0, 1]]
TAKES = ([(0, 0), (1, 0), (2, 0), (3, 0), (4, 0), (5, 0)], [(0, 1), (1, 1), (2, 1), (3, 1), (4, 1), (5, 1), (0, 2), (1, 2), (2, 2)])


def kernel(
    n, depth, height,
    v_hbm, w1_hbm, w2_hbm, c_hbm,
    resp_ref, g1_ref, g2_ref,
    vb, ab, cg, hg, w1_ref, w2_ref, conv, agr, hid,
    xts, xt, xtc, xvs, xv, xvc, part, bz, rz,
    ins,
    vs, vr, as_, ar, es, er, ts, tr, cs, cr, hs, hr, xs, xr, xes, xer, us, ur, sz, qz,
):
    rows, chans = v_hbm.shape[1:]
    quads = n // 4
    share = chans // n
    class_chans = chans // 4
    planes = 4 * depth
    duo = 2 * depth
    pad = height
    body = pl.ds(pad, rows)
    me = lax.axis_index("space")
    quad = me // 4
    q = lax.rem(me, 4)
    core = lax.rem(q, 2)
    side = q // 2
    mate = quad * 4 + q + 1 - 2 * lax.rem(q, 2)
    twin = quad * 4 + 3 - q
    across = quad * 4 + lax.rem(q + 2, 4)
    first = q * depth
    twin_first = (3 - q) * depth
    mate_first = (q + 1 - 2 * lax.rem(q, 2)) * depth
    across_first = lax.rem(q + 2, 4) * depth

    def remote(src, dst, send, recv, target):
        return pltpu.make_async_remote_copy(
            src_ref=src, dst_ref=dst, send_sem=send, recv_sem=recv,
            device_id={"space": target}, device_id_type=pl.DeviceIdType.MESH,
        )

    load_v = pltpu.make_async_copy(v_hbm, vb.at[pl.ds(1, depth), body], ins.at[0])
    load_c = pltpu.make_async_copy(c_hbm, cg.at[pl.ds(1 + first, depth), body], ins.at[1])
    load_w1 = pltpu.make_async_copy(w1_hbm, w1_ref, ins.at[2])
    load_w2 = pltpu.make_async_copy(w2_hbm, w2_ref, ins.at[3])
    barrier = pltpu.get_barrier_semaphore()
    for d in range(1, n):
        pl.semaphore_signal(
            barrier, inc=1, device_id={"space": lax.rem(me + d, n)},
            device_id_type=pl.DeviceIdType.MESH,
        )
    for copy in (load_v, load_c, load_w1, load_w2):
        copy.start()

    edge = jnp.zeros((pad, chans), BF16)
    for ref in (vb, ab, cg, hg):
        for p in range(ref.shape[0]):
            ref[p, :pad] = edge
            ref[p, pad + rows :] = edge
    plane_of_zeros = jnp.zeros((rows, chans), BF16)
    sliver = jnp.zeros((class_chans, rows), BF16)

    @pl.when(me == 0)
    def _():
        vb[0, body] = plane_of_zeros
        ab[0, body] = plane_of_zeros
        cg[0, body] = plane_of_zeros

    @pl.when(me == n - 1)
    def _():
        vb[depth + 1, body] = plane_of_zeros
        ab[depth + 1, body] = plane_of_zeros
        cg[planes + 1, body] = plane_of_zeros

    @pl.when(quad == 0)
    def _():
        xt[0] = sliver

    @pl.when(quad == quads - 1)
    def _():
        xt[planes + 1] = sliver

    pl.semaphore_wait(barrier, n - 1)

    def rims(low, high, ref, send, recv):
        up = remote(
            high, ref.at[0, body], send.at[0], recv.at[0], lax.rem(me + 1, n)
        )
        down = remote(
            low, ref.at[depth + 1, body], send.at[1], recv.at[1], lax.rem(me + n - 1, n)
        )
        return up, down

    def send_rims(up, down):
        @pl.when(me < n - 1)
        def _():
            up.start()

        @pl.when(me > 0)
        def _():
            down.start()

    def take_rims(up, down):
        @pl.when(me > 0)
        def _():
            up.wait_recv()

        @pl.when(me < n - 1)
        def _():
            down.wait_recv()

    def end_rims(up, down):
        @pl.when(me < n - 1)
        def _():
            up.wait_send()

        @pl.when(me > 0)
        def _():
            down.wait_send()

    v_rims = rims(v_hbm.at[0], v_hbm.at[depth - 1], vb, vs, vr)
    send_rims(*v_rims)

    c_up = remote(c_hbm.at[depth - 1], cg.at[0, body], es.at[0], er.at[0], lax.rem(me + 1, n))
    c_down = remote(
        c_hbm.at[0], cg.at[planes + 1, body], es.at[1], er.at[1], lax.rem(me + n - 1, n)
    )
    sends_up = (q == 3) & (quad < quads - 1)
    sends_down = (q == 0) & (quad > 0)

    @pl.when(sends_up)
    def _():
        c_up.start()

    @pl.when(sends_down)
    def _():
        c_down.start()

    def of_quad(start):
        return cg.at[pl.ds(1 + start, depth), body]

    def twin_plane(i):
        out = abs_order(side, i)
        back = abs_order(1 - side, i)
        there = cg.at[1 + first + out, body]
        here = cg.at[1 + twin_first + back, body]
        to = remote(c_hbm.at[out], there, ts.at[i], tr.at[i], twin)
        back_from = remote(c_hbm.at[out], here, ts.at[i], tr.at[i], twin)
        return to, back_from

    def abs_order(at_side, i):
        return (1 - at_side) * (depth - 1 - i) + at_side * i

    twin_planes = [twin_plane(i) for i in range(depth)]
    c_mate = remote(c_hbm, of_quad(first), cs.at[1], cr.at[1], mate)
    c_onward = remote(of_quad(twin_first), of_quad(twin_first), cs.at[2], cr.at[2], mate)
    c_from_mate = remote(c_hbm, of_quad(mate_first), cs.at[1], cr.at[1], mate)
    c_brought = remote(of_quad(across_first), of_quad(across_first), cs.at[2], cr.at[2], mate)
    beside_twin = (q == 1) | (q == 2)

    @pl.when(beside_twin)
    def _():
        twin_planes[0][0].start()

    c_mate.start()

    slot = lax.broadcasted_iota(jnp.int32, (chans, chans), 0)
    chan = lax.broadcasted_iota(jnp.int32, (chans, chans), 1)
    kind = slot // (2 * class_chans) + 2 * lax.rem(slot // class_chans, 2)
    inner = lax.rem(slot, class_chans)
    wanted = (4 * (inner // share) + kind) * share + lax.rem(inner, share)
    sorter = jnp.where(chan == wanted, 1.0, 0.0).astype(BF16)

    def turn(plane):
        return lax.dot_general(sorter, plane, NT, preferred_element_type=F32).astype(BF16)

    def class_of(device):
        return device - 4 * quad

    def act_slices():
        for p in range(depth):
            turned = turn(ab[1 + p, body])
            for j in range(4):
                top = (j % 2 * 2 + j // 2) * class_chans
                xts[j, p] = turned[top : top + class_chans]
        for j in range(4):
            up, down = sliver_to(j)

            @pl.when(sends_up)
            def _():
                up.start()

            @pl.when(sends_down)
            def _():
                down.start()

        for i, target in enumerate((twin, across, mate)):
            slice_to(i, target).start()
        for p in range(depth):
            xt[1 + first + p] = xts[q, p]

    def slice_to(i, target):
        return remote(
            xts.at[class_of(target)], xt.at[pl.ds(1 + first, depth)],
            xs.at[i], xr.at[i], target,
        )

    def slice_from(i, target):
        return remote(
            xts.at[class_of(target)], xt.at[pl.ds(1 + class_of(target) * depth, depth)],
            xs.at[i], xr.at[i], target,
        )

    def sliver_to(j):
        up = remote(
            xts.at[j, depth - 1], xt.at[0], xes.at[j], xer.at[0],
            lax.rem(quad + 1, quads) * 4 + j,
        )
        down = remote(
            xts.at[j, 0], xt.at[planes + 1], xes.at[j], xer.at[1],
            lax.rem(quad + quads - 1, quads) * 4 + j,
        )
        return up, down

    def take_slices():
        for i, target in enumerate((twin, across)):
            slice_from(i, target).wait_recv()
        up, down = sliver_to(0)

        @pl.when(quad > 0)
        def _():
            up.wait_recv()

        @pl.when(quad < quads - 1)
        def _():
            down.wait_recv()

    def end_slices():
        for i, target in enumerate((twin, across, mate)):
            slice_to(i, target).wait_send()
        for j in range(4):
            up, down = sliver_to(j)

            @pl.when(sends_up)
            def _():
                up.wait_send()

            @pl.when(sends_down)
            def _():
                down.wait_send()

    half = 2 * class_chans
    near = pl.ds(1 + core * depth, depth)
    far = pl.ds(1 + (1 - core) * depth, depth)
    near_rim = core * (duo + 1)
    far_rim = (1 - core) * (duo + 1)

    def vol_turn(p, plane):
        turned = turn(plane)
        for j in range(2):
            xvs[j, p] = turned[j * half : (j + 1) * half]

    v_mate = remote(xvs.at[1 - core, pl.ds(0, depth)], xv.at[near], us.at[0], ur.at[0], mate)
    v_from_mate = remote(xvs.at[1 - core, pl.ds(0, depth)], xv.at[far], us.at[0], ur.at[0], mate)
    v_rim_mate = remote(xvs.at[1 - core, depth], xv.at[near_rim], us.at[1], ur.at[1], mate)
    v_rim_from_mate = remote(xvs.at[1 - core, depth], xv.at[far_rim], us.at[1], ur.at[1], mate)

    h_near = hg.at[pl.ds(core * depth, depth), body]
    h_far = hg.at[pl.ds((1 - core) * depth, depth), body]
    h_mate = remote(h_near, h_near, hs.at[0], hr.at[0], mate)
    h_from_mate = remote(h_near, h_far, hs.at[0], hr.at[0], mate)

    def wide(ref, plane):
        return jnp.concatenate(
            [ref[plane, b * pad : b * pad + rows] for b in range(3)], axis=1
        )

    def w_first(a):
        return jnp.concatenate(
            [
                jnp.concatenate([w1_ref[a * 9 + b * 3 + c] for b in range(3)], axis=0)
                for c in range(3)
            ],
            axis=1,
        )

    def w_second(a):
        return jnp.concatenate(
            [
                jnp.concatenate([w2_ref[a * 9 + b * 3 + c] for b in range(3)], axis=0)
                for c in range(3)
            ],
            axis=1,
        )

    def w_turned(a):
        return jnp.concatenate(
            [
                jnp.concatenate([w2_ref[26 - (a * 9 + b * 3 + c)] for b in range(3)], axis=1)
                for c in range(3)
            ],
            axis=0,
        )

    def mul(x, w):
        return jnp.dot(x, w, preferred_element_type=F32)

    def mul_turned(x, w):
        return lax.dot_general(x, w, NT, preferred_element_type=F32)

    lane = lax.rem(lax.broadcasted_iota(jnp.int32, (rows, chans), 0), height)

    def fold(y):
        before = jnp.where(lane == 0, 0.0, pltpu.roll(y[:, :chans], 1, 0))
        after = jnp.where(lane == height - 1, 0.0, pltpu.roll(y[:, 2 * chans :], rows - 1, 0))
        return before + y[:, chans : 2 * chans] + after

    def inner_part(ref, base, w, product, acc):
        for p in range(depth):
            total = None
            for r in range(depth):
                a = r - p + 1
                if 0 <= a <= 2:
                    term = product(wide(ref, base + 1 + r), w(a))
                    total = term if total is None else total + term
            acc[p] = total

    def outer_part(ref, base, w, product, acc):
        low = acc[0] + product(wide(ref, base), w(0))
        if depth == 1:
            return (low + product(wide(ref, base + 2), w(2)),)
        mids = tuple(acc[p] for p in range(1, depth - 1))
        high = acc[depth - 1] + product(wide(ref, base + depth + 1), w(2))
        return (low,) + mids + (high,)

    step = lax.rem(lax.broadcasted_iota(jnp.int32, (class_chans, rows), 1), height)

    def shift_slices(src, dst, slots, tall):
        for slot in slots:
            cols = pl.ds(pl.multiple_of(slot * rows, rows), rows)
            for i in range(tall // class_chans):
                x = src[slot, i * class_chans : (i + 1) * class_chans]
                w = x.astype(F32)
                before = jnp.where(step == 0, 0.0, pltpu.roll(w, 1, 1)).astype(BF16)
                after = jnp.where(step == height - 1, 0.0, pltpu.roll(w, rows - 1, 1)).astype(BF16)
                for c, moved in enumerate((before, x, after)):
                    top = c * tall + i * class_chans
                    dst[top : top + class_chans, cols] = moved

    load_v.wait()
    for p in range(depth):
        vol_turn(p, vb[1 + p, body])
        xv[1 + core * depth + p] = xvs[core, p]
    v_mate.start()
    load_w1.wait()
    inner_part(vb, 0, w_first, mul, conv)
    @pl.when(jnp.logical_not(beside_twin))
    def _():
        twin_planes[0][0].start()

    for to, _ in twin_planes[1:]:
        to.start()
    load_c.wait()
    load_w2.wait()
    inner_part(cg, first, w_turned, mul_turned, agr)
    v_from_mate.wait_recv()
    shift_slices(xv, xvc, range(1, duo + 1), half)

    take_rims(*v_rims)
    for p, y in enumerate(outer_part(vb, 0, w_first, mul, conv)):
        h = fold(y)
        hid[p] = h
        ab[1 + p, body] = (h * jax.nn.sigmoid(h)).astype(BF16)
    act_slices()

    vol_turn(depth, vb[core * (depth + 1), body])
    xv[near_rim] = xvs[core, depth]
    v_rim_mate.start()

    @pl.when(beside_twin)
    def _():
        twin_planes[0][1].wait_recv()

    c_from_mate.wait_recv()

    @pl.when((q == 0) & (quad > 0))
    def _():
        c_up.wait_recv()

    @pl.when((q == 3) & (quad < quads - 1))
    def _():
        c_down.wait_recv()

    for p, y in enumerate(outer_part(cg, first, w_turned, mul_turned, agr)):
        h = hid[p]
        s = jax.nn.sigmoid(h)
        hg[core * depth + p, body] = (fold(y) * s * (1.0 + h * (1.0 - s))).astype(BF16)
    h_mate.start()

    def product_of(xs_ref, a, field, lead, count):
        taps = jnp.concatenate(
            [
                jnp.concatenate(
                    [field[lead + p, (2 - b) * pad : (2 - b) * pad + rows] for b in range(3)],
                    axis=1,
                )
                for p in range(count)
            ],
            axis=0,
        )
        return mul(xs_ref[:, a * rows : (a + count) * rows], taps)

    def bit(axis):
        return side if axis == "y" else lax.rem(quad // (1 << axis), 2)

    def partner(axis):
        if axis == "y":
            return across
        return (quad + (1 - 2 * bit(axis)) * (1 << axis)) * 4 + q

    levels = quads.bit_length() - 1
    axes = list(range(levels))[::-1]

    def plan(k):
        order = ORDERS[k] + [axis for axis in range(2, levels)]
        left = (["y"] if k < 3 else []) + axes
        steps, start = [], 0
        for axis in order:
            count = 1 << (len(left) - 1)
            stride = 1 << (len(left) - 1 - left.index(axis))
            steps.append((axis, count, stride, start))
            left.remove(axis)
            start += count
        return steps

    plans = [plan(k) for k in range(6)]

    def place(i, stride, which):
        return i // stride * 2 * stride + which * stride + i % stride

    def hop(k, level):
        axis, count, stride, start = plans[k][level]
        return remote(
            bz.at[k, pl.ds(start, count)], rz.at[k, pl.ds(start, count)],
            sz.at[k, level], qz.at[k, level], partner(axis),
        )

    def give(k, level):
        axis, count, stride, start = plans[k][level]
        for i in range(count):
            bz[k, start + i] = part[k, place(i, stride, 1 - bit(axis))].astype(BF16)
        hop(k, level).start()

    def take(k, level):
        axis, count, stride, start = plans[k][level]
        hop(k, level).wait_recv()
        for i in range(count):
            total = part[k, place(i, stride, bit(axis))] + rz[k, start + i].astype(F32)
            if level + 1 < len(plans[k]):
                part[k, i] = total
            else:
                (g1_ref, g2_ref)[k // 3][9 * (k % 3) : 9 * (k % 3) + 9] = total
        if level + 1 < len(plans[k]):
            give(k, level + 1)

    def first_piece(a):
        term = product_of(xvc, a, hg, 0, duo)
        for i in range(2):
            for z in range(quads):
                for b in range(3):
                    for c in range(3):
                        top = c * half + i * class_chans + z * share
                        part[a, i * quads + z, 3 * b + c] = term[
                            top : top + share, b * chans : (b + 1) * chans
                        ]
        give(a, 0)

    def second_piece(a):
        term = product_of(xtc, a, cg, 1, planes)
        for z in range(quads):
            for b in range(3):
                for c in range(3):
                    top = c * class_chans + z * share
                    part[3 + a, z, 3 * b + c] = term[
                        top : top + share, b * chans : (b + 1) * chans
                    ]
        give(3 + a, 0)

    v_rim_from_mate.wait_recv()
    shift_slices(xv, xvc, (0, duo + 1), half)
    h_from_mate.wait_recv()
    for a in range(3):
        first_piece(a)

    @pl.when(jnp.logical_not(beside_twin))
    def _():
        twin_planes[0][1].wait_recv()

    for _, back in twin_planes[1:]:
        back.wait_recv()
    c_onward.start()
    act_rims = rims(ab.at[1, body], ab.at[depth, body], ab, as_, ar)
    send_rims(*act_rims)

    shift_slices(xt, xtc, [1 + first + p for p in range(depth)], class_chans)
    slice_from(2, mate).wait_recv()
    shift_slices(xt, xtc, [1 + mate_first + p for p in range(depth)], class_chans)
    take_slices()
    rest = [1 + start + p for start in (twin_first, across_first) for p in range(depth)]
    shift_slices(xt, xtc, rest + [0, planes + 1], class_chans)
    c_brought.wait_recv()
    for a in range(3):
        second_piece(a)
    inner_part(ab, 0, w_second, mul, conv)
    for k, level in TAKES[0]:
        take(k, level)
    take_rims(*act_rims)
    for p, y in enumerate(outer_part(ab, 0, w_second, mul, conv)):
        resp_ref[p] = fold(y).astype(BF16)
    for k, level in TAKES[1]:
        take(k, level)
    for level in range(2, len(plans[0])):
        for k in range(6):
            if (k, level) not in TAKES[1] and level < len(plans[k]):
                take(k, level)

    end_rims(*v_rims)
    end_rims(*act_rims)

    @pl.when(sends_up)
    def _():
        c_up.wait_send()

    @pl.when(sends_down)
    def _():
        c_down.wait_send()

    for to, _ in twin_planes:
        to.wait_send()
    for copy in (c_mate, c_onward, v_mate, v_rim_mate, h_mate):
        copy.wait_send()
    end_slices()
    for k in range(6):
        for level in range(len(plans[k])):
            hop(k, level).wait_send()


def put(resp, g1, g2, resp_hbm, g1_hbm, g2_hbm, sems):
    pairs = ((resp, resp_hbm), (g1, g1_hbm), (g2, g2_hbm))
    copies = [pltpu.make_async_copy(src, dst, sems.at[i]) for i, (src, dst) in enumerate(pairs)]
    for copy in copies:
        copy.start()
    for copy in copies:
        copy.wait()


def per_device(n, volume, first_filter, second_filter, cotangent):
    depth, width, height, chans = volume.shape
    rows = width * height
    share = chans // n
    quads = n // 4
    planes = 4 * depth
    tall = rows + 2 * height
    class_chans = chans // 4
    levels = quads.bit_length() - 1
    dma = pltpu.SemaphoreType.DMA
    hbm = pl.BlockSpec(memory_space=pl.ANY)
    block = (27, share, chans)
    piece = (9, share, chans)
    vmem = pltpu.VMEM
    response, first, second = pl.pallas_call(
        functools.partial(kernel, n, depth, height),
        out_shape=(
            pltpu.VMEM((depth, rows, chans), BF16),
            pltpu.VMEM(block, F32),
            pltpu.VMEM(block, F32),
        ),
        in_specs=[hbm] * 4,
        out_specs=(pl.BlockSpec(memory_space=pltpu.VMEM),) * 3,
        scratch_shapes=[
            vmem((depth + 2, tall, chans), BF16),
            vmem((depth + 2, tall, chans), BF16),
            vmem((planes + 2, tall, chans), BF16),
            vmem((2 * depth, tall, chans), BF16),
            vmem((27, chans, chans), BF16),
            vmem((27, chans, chans), BF16),
            vmem((depth, rows, 3 * chans), F32),
            vmem((depth, rows, 3 * chans), F32),
            vmem((depth, rows, chans), F32),
            vmem((4, depth, class_chans, rows), BF16),
            vmem((planes + 2, class_chans, rows), BF16),
            vmem((3 * class_chans, (planes + 2) * rows), BF16),
            vmem((2, depth + 1, 2 * class_chans, rows), BF16),
            vmem((2 * depth + 2, 2 * class_chans, rows), BF16),
            vmem((6 * class_chans, (2 * depth + 2) * rows), BF16),
            vmem((6, 2 * quads) + piece, F32),
            vmem((6, 2 * quads) + piece, BF16),
            vmem((6, 2 * quads) + piece, BF16),
            dma((4,)),
            dma((2,)), dma((2,)), dma((2,)), dma((2,)), dma((2,)), dma((2,)),
            dma((depth,)), dma((depth,)), dma((3,)), dma((3,)), dma((1,)), dma((1,)),
            dma((3,)), dma((3,)), dma((4,)), dma((2,)), dma((2,)), dma((2,)),
            dma((6, levels + 1)), dma((6, levels + 1)),
        ],
        compiler_params=pltpu.CompilerParams(
            collective_id=0, has_side_effects=True, vmem_limit_bytes=58 * 1024 * 1024
        ),
    )(
        volume.reshape(depth, rows, chans),
        first_filter.reshape(27, chans, chans),
        second_filter.reshape(27, chans, chans),
        cotangent.reshape(depth, rows, chans),
    )
    response, first, second = pl.pallas_call(
        put,
        out_shape=(
            jax.ShapeDtypeStruct((depth, rows, chans), BF16),
            jax.ShapeDtypeStruct(block, F32),
            jax.ShapeDtypeStruct(block, F32),
        ),
        in_specs=[pl.BlockSpec(memory_space=pltpu.VMEM)] * 3,
        out_specs=(hbm,) * 3,
        scratch_shapes=[dma((3,))],
    )(*(pltpu.with_memory_space_constraint(x, pltpu.VMEM) for x in (response, first, second)))

    def laid(grad):
        return jnp.transpose(grad, (1, 0, 2)).reshape(share, 3, 3, 3, chans)

    return response.reshape(volume.shape), laid(first), laid(second)


def solution(mesh):
    n = mesh.shape["space"]
    field = P(("parts", "space"), None, None, None)
    grad = P(("parts", "space"), None, None, None, None)
    return jax.shard_map(
        functools.partial(per_device, n),
        mesh=mesh,
        in_specs=(field, P(), P(), field),
        out_specs=(field, grad, grad),
        check_vma=False,
    )
```

```python
import functools

import jax
import jax.numpy as jnp
from jax import lax
from jax.experimental import pallas as pl
from jax.experimental.pallas import tpu as pltpu
from jax.sharding import PartitionSpec as P

F32, BF16 = jnp.float32, jnp.bfloat16
NT = (((1,), (1,)), ((), ()))
ORDERS = [[0, 1, 'y'], ['y', 0, 1], ['y', 0, 1], [0, 1], [0, 1], [1, 0]]
TAKES = ([(0, 0), (1, 0), (2, 0), (3, 0), (4, 0), (5, 0)], [(0, 1), (1, 1), (2, 1), (3, 1), (4, 1), (5, 1), (0, 2), (1, 2), (2, 2)])


def kernel(
    n, depth, height,
    v_hbm, w1_hbm, w2_hbm, c_hbm,
    resp_ref, g1_ref, g2_ref,
    vb, ab, cg, hg, w1_ref, w2_ref, conv, agr, hid,
    xts, xt, xtc, xvs, xv, xvc, part, bz, rz,
    ins,
    vs, vr, as_, ar, es, er, ts, tr, cs, cr, hs, hr, xs, xr, xes, xer, us, ur, sz, qz,
):
    rows, chans = v_hbm.shape[1:]
    quads = n // 4
    share = chans // n
    class_chans = chans // 4
    planes = 4 * depth
    duo = 2 * depth
    pad = height
    body = pl.ds(pad, rows)
    me = lax.axis_index("space")
    quad = me // 4
    q = lax.rem(me, 4)
    core = lax.rem(q, 2)
    side = q // 2
    mate = quad * 4 + q + 1 - 2 * lax.rem(q, 2)
    twin = quad * 4 + 3 - q
    across = quad * 4 + lax.rem(q + 2, 4)
    first = q * depth
    twin_first = (3 - q) * depth
    mate_first = (q + 1 - 2 * lax.rem(q, 2)) * depth
    across_first = lax.rem(q + 2, 4) * depth

    def remote(src, dst, send, recv, target):
        return pltpu.make_async_remote_copy(
            src_ref=src, dst_ref=dst, send_sem=send, recv_sem=recv,
            device_id={"space": target}, device_id_type=pl.DeviceIdType.MESH,
        )

    load_v = pltpu.make_async_copy(v_hbm, vb.at[pl.ds(1, depth), body], ins.at[0])
    load_c = pltpu.make_async_copy(c_hbm, cg.at[pl.ds(1 + first, depth), body], ins.at[1])
    load_w1 = pltpu.make_async_copy(w1_hbm, w1_ref, ins.at[2])
    load_w2 = pltpu.make_async_copy(w2_hbm, w2_ref, ins.at[3])
    barrier = pltpu.get_barrier_semaphore()
    for d in range(1, n):
        pl.semaphore_signal(
            barrier, inc=1, device_id={"space": lax.rem(me + d, n)},
            device_id_type=pl.DeviceIdType.MESH,
        )
    for copy in (load_v, load_c, load_w1, load_w2):
        copy.start()

    edge = jnp.zeros((pad, chans), BF16)
    for ref in (vb, ab, cg, hg):
        for p in range(ref.shape[0]):
            ref[p, :pad] = edge
            ref[p, pad + rows :] = edge
    plane_of_zeros = jnp.zeros((rows, chans), BF16)
    sliver = jnp.zeros((class_chans, rows), BF16)

    @pl.when(me == 0)
    def _():
        vb[0, body] = plane_of_zeros
        ab[0, body] = plane_of_zeros
        cg[0, body] = plane_of_zeros

    @pl.when(me == n - 1)
    def _():
        vb[depth + 1, body] = plane_of_zeros
        ab[depth + 1, body] = plane_of_zeros
        cg[planes + 1, body] = plane_of_zeros

    @pl.when(quad == 0)
    def _():
        xt[0] = sliver

    @pl.when(quad == quads - 1)
    def _():
        xt[planes + 1] = sliver

    pl.semaphore_wait(barrier, n - 1)

    def rims(low, high, ref, send, recv):
        up = remote(
            high, ref.at[0, body], send.at[0], recv.at[0], lax.rem(me + 1, n)
        )
        down = remote(
            low, ref.at[depth + 1, body], send.at[1], recv.at[1], lax.rem(me + n - 1, n)
        )
        return up, down

    def send_rims(up, down):
        @pl.when(me < n - 1)
        def _():
            up.start()

        @pl.when(me > 0)
        def _():
            down.start()

    def take_rims(up, down):
        @pl.when(me > 0)
        def _():
            up.wait_recv()

        @pl.when(me < n - 1)
        def _():
            down.wait_recv()

    def end_rims(up, down):
        @pl.when(me < n - 1)
        def _():
            up.wait_send()

        @pl.when(me > 0)
        def _():
            down.wait_send()

    v_rims = rims(v_hbm.at[0], v_hbm.at[depth - 1], vb, vs, vr)
    send_rims(*v_rims)

    c_up = remote(c_hbm.at[depth - 1], cg.at[0, body], es.at[0], er.at[0], lax.rem(me + 1, n))
    c_down = remote(
        c_hbm.at[0], cg.at[planes + 1, body], es.at[1], er.at[1], lax.rem(me + n - 1, n)
    )
    sends_up = (q == 3) & (quad < quads - 1)
    sends_down = (q == 0) & (quad > 0)

    @pl.when(sends_up)
    def _():
        c_up.start()

    @pl.when(sends_down)
    def _():
        c_down.start()

    def of_quad(start):
        return cg.at[pl.ds(1 + start, depth), body]

    def twin_plane(i):
        out = abs_order(side, i)
        back = abs_order(1 - side, i)
        there = cg.at[1 + first + out, body]
        here = cg.at[1 + twin_first + back, body]
        to = remote(c_hbm.at[out], there, ts.at[i], tr.at[i], twin)
        back_from = remote(c_hbm.at[out], here, ts.at[i], tr.at[i], twin)
        return to, back_from

    def abs_order(at_side, i):
        return (1 - at_side) * (depth - 1 - i) + at_side * i

    twin_planes = [twin_plane(i) for i in range(depth)]
    c_mate = remote(c_hbm, of_quad(first), cs.at[0], cr.at[0], mate)

    def onward_plane(i):
        out = abs_order(1 - side, i)
        passed = cg.at[1 + twin_first + out, body]
        here = cg.at[1 + across_first + out, body]
        to = remote(passed, passed, cs.at[1 + i], cr.at[1 + i], mate)
        brought = remote(passed, here, cs.at[1 + i], cr.at[1 + i], mate)
        return to, brought

    onward_planes = [onward_plane(i) for i in range(depth)]
    c_from_mate = remote(c_hbm, of_quad(mate_first), cs.at[0], cr.at[0], mate)
    beside_twin = (q == 1) | (q == 2)

    @pl.when(beside_twin)
    def _():
        twin_planes[0][0].start()

    c_mate.start()

    slot = lax.broadcasted_iota(jnp.int32, (chans, chans), 0)
    chan = lax.broadcasted_iota(jnp.int32, (chans, chans), 1)
    kind = slot // (2 * class_chans) + 2 * lax.rem(slot // class_chans, 2)
    inner = lax.rem(slot, class_chans)
    wanted = (4 * (inner // share) + kind) * share + lax.rem(inner, share)
    sorter = jnp.where(chan == wanted, 1.0, 0.0).astype(BF16)

    def turn(plane):
        return lax.dot_general(sorter, plane, NT, preferred_element_type=F32).astype(BF16)

    def class_of(device):
        return device - 4 * quad

    def act_slices():
        for p in range(depth):
            turned = turn(ab[1 + p, body])
            for j in range(4):
                top = (j % 2 * 2 + j // 2) * class_chans
                xts[j, p] = turned[top : top + class_chans]
        for j in range(4):
            up, down = sliver_to(j)

            @pl.when(sends_up)
            def _():
                up.start()

            @pl.when(sends_down)
            def _():
                down.start()

        for i, target in enumerate((twin, across, mate)):
            slice_to(i, target).start()
        for p in range(depth):
            xt[1 + first + p] = xts[q, p]

    def slice_to(i, target):
        return remote(
            xts.at[class_of(target)], xt.at[pl.ds(1 + first, depth)],
            xs.at[i], xr.at[i], target,
        )

    def slice_from(i, target):
        return remote(
            xts.at[class_of(target)], xt.at[pl.ds(1 + class_of(target) * depth, depth)],
            xs.at[i], xr.at[i], target,
        )

    def sliver_to(j):
        up = remote(
            xts.at[j, depth - 1], xt.at[0], xes.at[j], xer.at[0],
            lax.rem(quad + 1, quads) * 4 + j,
        )
        down = remote(
            xts.at[j, 0], xt.at[planes + 1], xes.at[j], xer.at[1],
            lax.rem(quad + quads - 1, quads) * 4 + j,
        )
        return up, down

    def take_slices():
        for i, target in enumerate((twin, across)):
            slice_from(i, target).wait_recv()
        up, down = sliver_to(0)

        @pl.when(quad > 0)
        def _():
            up.wait_recv()

        @pl.when(quad < quads - 1)
        def _():
            down.wait_recv()

    def end_slices():
        for i, target in enumerate((twin, across, mate)):
            slice_to(i, target).wait_send()
        for j in range(4):
            up, down = sliver_to(j)

            @pl.when(sends_up)
            def _():
                up.wait_send()

            @pl.when(sends_down)
            def _():
                down.wait_send()

    half = 2 * class_chans
    near = pl.ds(1 + core * depth, depth)
    far = pl.ds(1 + (1 - core) * depth, depth)
    near_rim = core * (duo + 1)
    far_rim = (1 - core) * (duo + 1)

    def vol_turn(p, plane):
        turned = turn(plane)
        for j in range(2):
            xvs[j, p] = turned[j * half : (j + 1) * half]

    v_mate = remote(xvs.at[1 - core, pl.ds(0, depth)], xv.at[near], us.at[0], ur.at[0], mate)
    v_from_mate = remote(xvs.at[1 - core, pl.ds(0, depth)], xv.at[far], us.at[0], ur.at[0], mate)
    v_rim_mate = remote(xvs.at[1 - core, depth], xv.at[near_rim], us.at[1], ur.at[1], mate)
    v_rim_from_mate = remote(xvs.at[1 - core, depth], xv.at[far_rim], us.at[1], ur.at[1], mate)

    h_near = hg.at[pl.ds(core * depth, depth), body]
    h_far = hg.at[pl.ds((1 - core) * depth, depth), body]
    h_mate = remote(h_near, h_near, hs.at[0], hr.at[0], mate)
    h_from_mate = remote(h_near, h_far, hs.at[0], hr.at[0], mate)

    def wide(ref, plane):
        return jnp.concatenate(
            [ref[plane, b * pad : b * pad + rows] for b in range(3)], axis=1
        )

    def w_first(a):
        return jnp.concatenate(
            [
                jnp.concatenate([w1_ref[a * 9 + b * 3 + c] for b in range(3)], axis=0)
                for c in range(3)
            ],
            axis=1,
        )

    def w_second(a):
        return jnp.concatenate(
            [
                jnp.concatenate([w2_ref[a * 9 + b * 3 + c] for b in range(3)], axis=0)
                for c in range(3)
            ],
            axis=1,
        )

    def w_turned(a):
        return jnp.concatenate(
            [
                jnp.concatenate([w2_ref[26 - (a * 9 + b * 3 + c)] for b in range(3)], axis=1)
                for c in range(3)
            ],
            axis=0,
        )

    def mul(x, w):
        return jnp.dot(x, w, preferred_element_type=F32)

    def mul_turned(x, w):
        return lax.dot_general(x, w, NT, preferred_element_type=F32)

    lane = lax.rem(lax.broadcasted_iota(jnp.int32, (rows, chans), 0), height)

    def fold(y):
        before = jnp.where(lane == 0, 0.0, pltpu.roll(y[:, :chans], 1, 0))
        after = jnp.where(lane == height - 1, 0.0, pltpu.roll(y[:, 2 * chans :], rows - 1, 0))
        return before + y[:, chans : 2 * chans] + after

    def inner_part(ref, base, w, product, acc):
        for p in range(depth):
            total = None
            for r in range(depth):
                a = r - p + 1
                if 0 <= a <= 2:
                    term = product(wide(ref, base + 1 + r), w(a))
                    total = term if total is None else total + term
            acc[p] = total

    def outer_part(ref, base, w, product, acc):
        low = acc[0] + product(wide(ref, base), w(0))
        if depth == 1:
            return (low + product(wide(ref, base + 2), w(2)),)
        mids = tuple(acc[p] for p in range(1, depth - 1))
        high = acc[depth - 1] + product(wide(ref, base + depth + 1), w(2))
        return (low,) + mids + (high,)

    step = lax.rem(lax.broadcasted_iota(jnp.int32, (class_chans, rows), 1), height)

    def shift_slices(src, dst, slots, tall):
        for slot in slots:
            cols = pl.ds(pl.multiple_of(slot * rows, rows), rows)
            for i in range(tall // class_chans):
                x = src[slot, i * class_chans : (i + 1) * class_chans]
                w = x.astype(F32)
                before = jnp.where(step == 0, 0.0, pltpu.roll(w, 1, 1)).astype(BF16)
                after = jnp.where(step == height - 1, 0.0, pltpu.roll(w, rows - 1, 1)).astype(BF16)
                for c, moved in enumerate((before, x, after)):
                    top = c * tall + i * class_chans
                    dst[top : top + class_chans, cols] = moved

    load_v.wait()
    for p in range(depth):
        vol_turn(p, vb[1 + p, body])
        xv[1 + core * depth + p] = xvs[core, p]
    v_mate.start()
    load_w1.wait()
    inner_part(vb, 0, w_first, mul, conv)
    @pl.when(jnp.logical_not(beside_twin))
    def _():
        twin_planes[0][0].start()

    for to, _ in twin_planes[1:]:
        to.start()
    load_c.wait()
    load_w2.wait()
    inner_part(cg, first, w_turned, mul_turned, agr)
    v_from_mate.wait_recv()
    shift_slices(xv, xvc, range(1, duo + 1), half)

    take_rims(*v_rims)
    for p, y in enumerate(outer_part(vb, 0, w_first, mul, conv)):
        h = fold(y)
        hid[p] = h
        ab[1 + p, body] = (h * jax.nn.sigmoid(h)).astype(BF16)
    act_slices()

    vol_turn(depth, vb[core * (depth + 1), body])
    xv[near_rim] = xvs[core, depth]
    v_rim_mate.start()

    @pl.when(beside_twin)
    def _():
        twin_planes[0][1].wait_recv()
        onward_planes[0][0].start()

    c_from_mate.wait_recv()

    @pl.when((q == 0) & (quad > 0))
    def _():
        c_up.wait_recv()

    @pl.when((q == 3) & (quad < quads - 1))
    def _():
        c_down.wait_recv()

    for p, y in enumerate(outer_part(cg, first, w_turned, mul_turned, agr)):
        h = hid[p]
        s = jax.nn.sigmoid(h)
        hg[core * depth + p, body] = (fold(y) * s * (1.0 + h * (1.0 - s))).astype(BF16)
    h_mate.start()

    def product_of(xs_ref, a, field, lead, count):
        taps = jnp.concatenate(
            [
                jnp.concatenate(
                    [field[lead + p, (2 - b) * pad : (2 - b) * pad + rows] for b in range(3)],
                    axis=1,
                )
                for p in range(count)
            ],
            axis=0,
        )
        return mul(xs_ref[:, a * rows : (a + count) * rows], taps)

    def bit(axis):
        return side if axis == "y" else lax.rem(quad // (1 << axis), 2)

    def partner(axis):
        if axis == "y":
            return across
        return (quad + (1 - 2 * bit(axis)) * (1 << axis)) * 4 + q

    levels = quads.bit_length() - 1
    axes = list(range(levels))[::-1]

    def plan(k):
        order = ORDERS[k] + [axis for axis in range(2, levels)]
        left = (["y"] if k < 3 else []) + axes
        steps, start = [], 0
        for axis in order:
            count = 1 << (len(left) - 1)
            stride = 1 << (len(left) - 1 - left.index(axis))
            steps.append((axis, count, stride, start))
            left.remove(axis)
            start += count
        return steps

    plans = [plan(k) for k in range(6)]

    def place(i, stride, which):
        return i // stride * 2 * stride + which * stride + i % stride

    def hop(k, level):
        axis, count, stride, start = plans[k][level]
        return remote(
            bz.at[k, pl.ds(start, count)], rz.at[k, pl.ds(start, count)],
            sz.at[k, level], qz.at[k, level], partner(axis),
        )

    def give(k, level):
        axis, count, stride, start = plans[k][level]
        for i in range(count):
            bz[k, start + i] = part[k, place(i, stride, 1 - bit(axis))].astype(BF16)
        hop(k, level).start()

    def take(k, level):
        axis, count, stride, start = plans[k][level]
        hop(k, level).wait_recv()
        for i in range(count):
            total = part[k, place(i, stride, bit(axis))] + rz[k, start + i].astype(F32)
            if level + 1 < len(plans[k]):
                part[k, i] = total
            else:
                (g1_ref, g2_ref)[k // 3][9 * (k % 3) : 9 * (k % 3) + 9] = total
        if level + 1 < len(plans[k]):
            give(k, level + 1)

    def first_piece(a):
        term = product_of(xvc, a, hg, 0, duo)
        for i in range(2):
            for z in range(quads):
                for b in range(3):
                    for c in range(3):
                        top = c * half + i * class_chans + z * share
                        part[a, i * quads + z, 3 * b + c] = term[
                            top : top + share, b * chans : (b + 1) * chans
                        ]
        give(a, 0)

    def second_piece(a):
        term = product_of(xtc, a, cg, 1, planes)
        for z in range(quads):
            for b in range(3):
                for c in range(3):
                    top = c * class_chans + z * share
                    part[3 + a, z, 3 * b + c] = term[
                        top : top + share, b * chans : (b + 1) * chans
                    ]
        give(3 + a, 0)

    v_rim_from_mate.wait_recv()
    shift_slices(xv, xvc, (0, duo + 1), half)
    h_from_mate.wait_recv()
    for a in range(3):
        first_piece(a)

    @pl.when(jnp.logical_not(beside_twin))
    def _():
        twin_planes[0][1].wait_recv()
        onward_planes[0][0].start()

    for i in range(1, depth):
        twin_planes[i][1].wait_recv()
        onward_planes[i][0].start()
    act_rims = rims(ab.at[1, body], ab.at[depth, body], ab, as_, ar)
    send_rims(*act_rims)

    shift_slices(xt, xtc, [1 + first + p for p in range(depth)], class_chans)
    slice_from(2, mate).wait_recv()
    shift_slices(xt, xtc, [1 + mate_first + p for p in range(depth)], class_chans)
    take_slices()
    rest = [1 + start + p for start in (twin_first, across_first) for p in range(depth)]
    shift_slices(xt, xtc, rest + [0, planes + 1], class_chans)
    for _, brought in onward_planes:
        brought.wait_recv()
    for a in range(3):
        second_piece(a)
    inner_part(ab, 0, w_second, mul, conv)
    for k, level in TAKES[0]:
        take(k, level)
    take_rims(*act_rims)
    for p, y in enumerate(outer_part(ab, 0, w_second, mul, conv)):
        resp_ref[p] = fold(y).astype(BF16)
    for k, level in TAKES[1]:
        take(k, level)
    for level in range(2, len(plans[0])):
        for k in range(6):
            if (k, level) not in TAKES[1] and level < len(plans[k]):
                take(k, level)

    end_rims(*v_rims)
    end_rims(*act_rims)

    @pl.when(sends_up)
    def _():
        c_up.wait_send()

    @pl.when(sends_down)
    def _():
        c_down.wait_send()

    for to, _ in twin_planes + onward_planes:
        to.wait_send()
    for copy in (c_mate, v_mate, v_rim_mate, h_mate):
        copy.wait_send()
    end_slices()
    for k in range(6):
        for level in range(len(plans[k])):
            hop(k, level).wait_send()


def put(resp, g1, g2, resp_hbm, g1_hbm, g2_hbm, sems):
    pairs = ((resp, resp_hbm), (g1, g1_hbm), (g2, g2_hbm))
    copies = [pltpu.make_async_copy(src, dst, sems.at[i]) for i, (src, dst) in enumerate(pairs)]
    for copy in copies:
        copy.start()
    for copy in copies:
        copy.wait()


def per_device(n, volume, first_filter, second_filter, cotangent):
    depth, width, height, chans = volume.shape
    rows = width * height
    share = chans // n
    quads = n // 4
    planes = 4 * depth
    tall = rows + 2 * height
    class_chans = chans // 4
    levels = quads.bit_length() - 1
    dma = pltpu.SemaphoreType.DMA
    hbm = pl.BlockSpec(memory_space=pl.ANY)
    block = (27, share, chans)
    piece = (9, share, chans)
    vmem = pltpu.VMEM
    response, first, second = pl.pallas_call(
        functools.partial(kernel, n, depth, height),
        out_shape=(
            pltpu.VMEM((depth, rows, chans), BF16),
            pltpu.VMEM(block, F32),
            pltpu.VMEM(block, F32),
        ),
        in_specs=[hbm] * 4,
        out_specs=(pl.BlockSpec(memory_space=pltpu.VMEM),) * 3,
        scratch_shapes=[
            vmem((depth + 2, tall, chans), BF16),
            vmem((depth + 2, tall, chans), BF16),
            vmem((planes + 2, tall, chans), BF16),
            vmem((2 * depth, tall, chans), BF16),
            vmem((27, chans, chans), BF16),
            vmem((27, chans, chans), BF16),
            vmem((depth, rows, 3 * chans), F32),
            vmem((depth, rows, 3 * chans), F32),
            vmem((depth, rows, chans), F32),
            vmem((4, depth, class_chans, rows), BF16),
            vmem((planes + 2, class_chans, rows), BF16),
            vmem((3 * class_chans, (planes + 2) * rows), BF16),
            vmem((2, depth + 1, 2 * class_chans, rows), BF16),
            vmem((2 * depth + 2, 2 * class_chans, rows), BF16),
            vmem((6 * class_chans, (2 * depth + 2) * rows), BF16),
            vmem((6, 2 * quads) + piece, F32),
            vmem((6, 2 * quads) + piece, BF16),
            vmem((6, 2 * quads) + piece, BF16),
            dma((4,)),
            dma((2,)), dma((2,)), dma((2,)), dma((2,)), dma((2,)), dma((2,)),
            dma((depth,)), dma((depth,)), dma((1 + depth,)), dma((1 + depth,)), dma((1,)), dma((1,)),
            dma((3,)), dma((3,)), dma((4,)), dma((2,)), dma((2,)), dma((2,)),
            dma((6, levels + 1)), dma((6, levels + 1)),
        ],
        compiler_params=pltpu.CompilerParams(
            collective_id=0, has_side_effects=True, vmem_limit_bytes=58 * 1024 * 1024
        ),
    )(
        volume.reshape(depth, rows, chans),
        first_filter.reshape(27, chans, chans),
        second_filter.reshape(27, chans, chans),
        cotangent.reshape(depth, rows, chans),
    )
    response, first, second = pl.pallas_call(
        put,
        out_shape=(
            jax.ShapeDtypeStruct((depth, rows, chans), BF16),
            jax.ShapeDtypeStruct(block, F32),
            jax.ShapeDtypeStruct(block, F32),
        ),
        in_specs=[pl.BlockSpec(memory_space=pltpu.VMEM)] * 3,
        out_specs=(hbm,) * 3,
        scratch_shapes=[dma((3,))],
    )(*(pltpu.with_memory_space_constraint(x, pltpu.VMEM) for x in (response, first, second)))

    def laid(grad):
        return jnp.transpose(grad, (1, 0, 2)).reshape(share, 3, 3, 3, chans)

    return response.reshape(volume.shape), laid(first), laid(second)


def solution(mesh):
    n = mesh.shape["space"]
    field = P(("parts", "space"), None, None, None)
    grad = P(("parts", "space"), None, None, None, None)
    return jax.shard_map(
        functools.partial(per_device, n),
        mesh=mesh,
        in_specs=(field, P(), P(), field),
        out_specs=(field, grad, grad),
        check_vma=False,
    )
```

```python
import functools

import jax
import jax.numpy as jnp
from jax import lax
from jax.experimental import pallas as pl
from jax.experimental.pallas import tpu as pltpu
from jax.sharding import PartitionSpec as P

F32, BF16 = jnp.float32, jnp.bfloat16
NT = (((1,), (1,)), ((), ()))
ORDERS = [[0, 1, 'y'], ['y', 0, 1], ['y', 0, 1], [0, 1], [0, 1], [1, 0]]
TAKES = ([(0, 0), (1, 0), (2, 0), (3, 0), (4, 0), (5, 0)], [(0, 1), (1, 1), (2, 1), (3, 1), (4, 1), (5, 1), (0, 2), (1, 2), (2, 2)])


def kernel(
    n, depth, height,
    v_hbm, w1_hbm, w2_hbm, c_hbm,
    resp_ref, g1_ref, g2_ref,
    vb, ab, cg, hg, w1_ref, w2_ref, conv, agr, hid,
    xts, xt, xtc, xvs, xv, xvc, part, bz, rz,
    ins,
    vs, vr, as_, ar, es, er, ts, tr, cs, cr, hs, hr, xs, xr, xes, xer, us, ur, sz, qz,
):
    rows, chans = v_hbm.shape[1:]
    quads = n // 4
    share = chans // n
    class_chans = chans // 4
    planes = 4 * depth
    duo = 2 * depth
    pad = height
    body = pl.ds(pad, rows)
    me = lax.axis_index("space")
    quad = me // 4
    q = lax.rem(me, 4)
    core = lax.rem(q, 2)
    side = q // 2
    mate = quad * 4 + q + 1 - 2 * lax.rem(q, 2)
    twin = quad * 4 + 3 - q
    across = quad * 4 + lax.rem(q + 2, 4)
    first = q * depth
    twin_first = (3 - q) * depth
    mate_first = (q + 1 - 2 * lax.rem(q, 2)) * depth
    across_first = lax.rem(q + 2, 4) * depth

    def remote(src, dst, send, recv, target):
        return pltpu.make_async_remote_copy(
            src_ref=src, dst_ref=dst, send_sem=send, recv_sem=recv,
            device_id={"space": target}, device_id_type=pl.DeviceIdType.MESH,
        )

    load_v = pltpu.make_async_copy(v_hbm, vb.at[pl.ds(1, depth), body], ins.at[0])
    load_c = pltpu.make_async_copy(c_hbm, cg.at[pl.ds(1 + first, depth), body], ins.at[1])
    load_w1 = pltpu.make_async_copy(w1_hbm, w1_ref, ins.at[2])
    load_w2 = pltpu.make_async_copy(w2_hbm, w2_ref, ins.at[3])
    barrier = pltpu.get_barrier_semaphore()
    for d in range(1, n):
        pl.semaphore_signal(
            barrier, inc=1, device_id={"space": lax.rem(me + d, n)},
            device_id_type=pl.DeviceIdType.MESH,
        )
    for copy in (load_v, load_c, load_w1, load_w2):
        copy.start()

    pl.semaphore_wait(barrier, n - 1)

    def rims(low, high, ref, send, recv):
        up = remote(
            high, ref.at[0, body], send.at[0], recv.at[0], lax.rem(me + 1, n)
        )
        down = remote(
            low, ref.at[depth + 1, body], send.at[1], recv.at[1], lax.rem(me + n - 1, n)
        )
        return up, down

    def send_rims(up, down):
        @pl.when(me < n - 1)
        def _():
            up.start()

        @pl.when(me > 0)
        def _():
            down.start()

    def take_rims(up, down):
        @pl.when(me > 0)
        def _():
            up.wait_recv()

        @pl.when(me < n - 1)
        def _():
            down.wait_recv()

    def end_rims(up, down):
        @pl.when(me < n - 1)
        def _():
            up.wait_send()

        @pl.when(me > 0)
        def _():
            down.wait_send()

    v_rims = rims(v_hbm.at[0], v_hbm.at[depth - 1], vb, vs, vr)
    send_rims(*v_rims)

    c_up = remote(c_hbm.at[depth - 1], cg.at[0, body], es.at[0], er.at[0], lax.rem(me + 1, n))
    c_down = remote(
        c_hbm.at[0], cg.at[planes + 1, body], es.at[1], er.at[1], lax.rem(me + n - 1, n)
    )
    sends_up = (q == 3) & (quad < quads - 1)
    sends_down = (q == 0) & (quad > 0)

    @pl.when(sends_up)
    def _():
        c_up.start()

    @pl.when(sends_down)
    def _():
        c_down.start()

    edge = jnp.zeros((pad, chans), BF16)
    for ref in (vb, ab, cg, hg):
        for p in range(ref.shape[0]):
            ref[p, :pad] = edge
            ref[p, pad + rows :] = edge
    plane_of_zeros = jnp.zeros((rows, chans), BF16)
    sliver = jnp.zeros((class_chans, rows), BF16)

    @pl.when(me == 0)
    def _():
        vb[0, body] = plane_of_zeros
        ab[0, body] = plane_of_zeros
        cg[0, body] = plane_of_zeros

    @pl.when(me == n - 1)
    def _():
        vb[depth + 1, body] = plane_of_zeros
        ab[depth + 1, body] = plane_of_zeros
        cg[planes + 1, body] = plane_of_zeros

    @pl.when(quad == 0)
    def _():
        xt[0] = sliver

    @pl.when(quad == quads - 1)
    def _():
        xt[planes + 1] = sliver

    def of_quad(start):
        return cg.at[pl.ds(1 + start, depth), body]

    def twin_plane(i):
        out = abs_order(side, i)
        back = abs_order(1 - side, i)
        there = cg.at[1 + first + out, body]
        here = cg.at[1 + twin_first + back, body]
        to = remote(c_hbm.at[out], there, ts.at[i], tr.at[i], twin)
        back_from = remote(c_hbm.at[out], here, ts.at[i], tr.at[i], twin)
        return to, back_from

    def abs_order(at_side, i):
        return (1 - at_side) * (depth - 1 - i) + at_side * i

    twin_planes = [twin_plane(i) for i in range(depth)]
    c_mate = remote(c_hbm, of_quad(first), cs.at[0], cr.at[0], mate)

    def onward_plane(i):
        out = abs_order(1 - side, i)
        passed = cg.at[1 + twin_first + out, body]
        here = cg.at[1 + across_first + out, body]
        to = remote(passed, passed, cs.at[1 + i], cr.at[1 + i], mate)
        brought = remote(passed, here, cs.at[1 + i], cr.at[1 + i], mate)
        return to, brought

    onward_planes = [onward_plane(i) for i in range(depth)]
    c_from_mate = remote(c_hbm, of_quad(mate_first), cs.at[0], cr.at[0], mate)
    beside_twin = (q == 1) | (q == 2)

    @pl.when(beside_twin)
    def _():
        twin_planes[0][0].start()

    c_mate.start()

    slot = lax.broadcasted_iota(jnp.int32, (chans, chans), 0)
    chan = lax.broadcasted_iota(jnp.int32, (chans, chans), 1)
    kind = slot // (2 * class_chans) + 2 * lax.rem(slot // class_chans, 2)
    inner = lax.rem(slot, class_chans)
    wanted = (4 * (inner // share) + kind) * share + lax.rem(inner, share)
    sorter = jnp.where(chan == wanted, 1.0, 0.0).astype(BF16)

    def turn(plane):
        return lax.dot_general(sorter, plane, NT, preferred_element_type=F32).astype(BF16)

    def class_of(device):
        return device - 4 * quad

    def act_slices():
        for p in range(depth):
            turned = turn(ab[1 + p, body])
            for j in range(4):
                top = (j % 2 * 2 + j // 2) * class_chans
                xts[j, p] = turned[top : top + class_chans]
        for j in range(4):
            up, down = sliver_to(j)

            @pl.when(sends_up)
            def _():
                up.start()

            @pl.when(sends_down)
            def _():
                down.start()

        for i, target in enumerate((twin, across, mate)):
            slice_to(i, target).start()
        for p in range(depth):
            xt[1 + first + p] = xts[q, p]

    def slice_to(i, target):
        return remote(
            xts.at[class_of(target)], xt.at[pl.ds(1 + first, depth)],
            xs.at[i], xr.at[i], target,
        )

    def slice_from(i, target):
        return remote(
            xts.at[class_of(target)], xt.at[pl.ds(1 + class_of(target) * depth, depth)],
            xs.at[i], xr.at[i], target,
        )

    def sliver_to(j):
        up = remote(
            xts.at[j, depth - 1], xt.at[0], xes.at[j], xer.at[0],
            lax.rem(quad + 1, quads) * 4 + j,
        )
        down = remote(
            xts.at[j, 0], xt.at[planes + 1], xes.at[j], xer.at[1],
            lax.rem(quad + quads - 1, quads) * 4 + j,
        )
        return up, down

    def take_slices():
        for i, target in enumerate((twin, across)):
            slice_from(i, target).wait_recv()
        up, down = sliver_to(0)

        @pl.when(quad > 0)
        def _():
            up.wait_recv()

        @pl.when(quad < quads - 1)
        def _():
            down.wait_recv()

    def end_slices():
        for i, target in enumerate((twin, across, mate)):
            slice_to(i, target).wait_send()
        for j in range(4):
            up, down = sliver_to(j)

            @pl.when(sends_up)
            def _():
                up.wait_send()

            @pl.when(sends_down)
            def _():
                down.wait_send()

    half = 2 * class_chans
    near = pl.ds(1 + core * depth, depth)
    far = pl.ds(1 + (1 - core) * depth, depth)
    near_rim = core * (duo + 1)
    far_rim = (1 - core) * (duo + 1)

    def vol_turn(p, plane):
        turned = turn(plane)
        for j in range(2):
            xvs[j, p] = turned[j * half : (j + 1) * half]

    v_mate = remote(xvs.at[1 - core, pl.ds(0, depth)], xv.at[near], us.at[0], ur.at[0], mate)
    v_from_mate = remote(xvs.at[1 - core, pl.ds(0, depth)], xv.at[far], us.at[0], ur.at[0], mate)
    v_rim_mate = remote(xvs.at[1 - core, depth], xv.at[near_rim], us.at[1], ur.at[1], mate)
    v_rim_from_mate = remote(xvs.at[1 - core, depth], xv.at[far_rim], us.at[1], ur.at[1], mate)

    h_near = hg.at[pl.ds(core * depth, depth), body]
    h_far = hg.at[pl.ds((1 - core) * depth, depth), body]
    h_mate = remote(h_near, h_near, hs.at[0], hr.at[0], mate)
    h_from_mate = remote(h_near, h_far, hs.at[0], hr.at[0], mate)

    def wide(ref, plane):
        return jnp.concatenate(
            [ref[plane, b * pad : b * pad + rows] for b in range(3)], axis=1
        )

    def w_first(a):
        return jnp.concatenate(
            [
                jnp.concatenate([w1_ref[a * 9 + b * 3 + c] for b in range(3)], axis=0)
                for c in range(3)
            ],
            axis=1,
        )

    def w_second(a):
        return jnp.concatenate(
            [
                jnp.concatenate([w2_ref[a * 9 + b * 3 + c] for b in range(3)], axis=0)
                for c in range(3)
            ],
            axis=1,
        )

    def w_turned(a):
        return jnp.concatenate(
            [
                jnp.concatenate([w2_ref[26 - (a * 9 + b * 3 + c)] for b in range(3)], axis=1)
                for c in range(3)
            ],
            axis=0,
        )

    def mul(x, w):
        return jnp.dot(x, w, preferred_element_type=F32)

    def mul_turned(x, w):
        return lax.dot_general(x, w, NT, preferred_element_type=F32)

    lane = lax.rem(lax.broadcasted_iota(jnp.int32, (rows, chans), 0), height)

    def fold(y):
        before = jnp.where(lane == 0, 0.0, pltpu.roll(y[:, :chans], 1, 0))
        after = jnp.where(lane == height - 1, 0.0, pltpu.roll(y[:, 2 * chans :], rows - 1, 0))
        return before + y[:, chans : 2 * chans] + after

    def inner_part(ref, base, w, product, acc):
        for p in range(depth):
            total = None
            for r in range(depth):
                a = r - p + 1
                if 0 <= a <= 2:
                    term = product(wide(ref, base + 1 + r), w(a))
                    total = term if total is None else total + term
            acc[p] = total

    def outer_part(ref, base, w, product, acc):
        low = acc[0] + product(wide(ref, base), w(0))
        if depth == 1:
            return (low + product(wide(ref, base + 2), w(2)),)
        mids = tuple(acc[p] for p in range(1, depth - 1))
        high = acc[depth - 1] + product(wide(ref, base + depth + 1), w(2))
        return (low,) + mids + (high,)

    step = lax.rem(lax.broadcasted_iota(jnp.int32, (class_chans, rows), 1), height)

    def shift_slices(src, dst, slots, tall):
        for slot in slots:
            cols = pl.ds(pl.multiple_of(slot * rows, rows), rows)
            for i in range(tall // class_chans):
                x = src[slot, i * class_chans : (i + 1) * class_chans]
                w = x.astype(F32)
                before = jnp.where(step == 0, 0.0, pltpu.roll(w, 1, 1)).astype(BF16)
                after = jnp.where(step == height - 1, 0.0, pltpu.roll(w, rows - 1, 1)).astype(BF16)
                for c, moved in enumerate((before, x, after)):
                    top = c * tall + i * class_chans
                    dst[top : top + class_chans, cols] = moved

    load_v.wait()
    for p in range(depth):
        vol_turn(p, vb[1 + p, body])
        xv[1 + core * depth + p] = xvs[core, p]
    v_mate.start()
    load_w1.wait()
    inner_part(vb, 0, w_first, mul, conv)
    @pl.when(jnp.logical_not(beside_twin))
    def _():
        twin_planes[0][0].start()

    for to, _ in twin_planes[1:]:
        to.start()
    load_c.wait()
    load_w2.wait()
    inner_part(cg, first, w_turned, mul_turned, agr)
    v_from_mate.wait_recv()
    shift_slices(xv, xvc, range(1, duo + 1), half)

    take_rims(*v_rims)
    for p, y in enumerate(outer_part(vb, 0, w_first, mul, conv)):
        h = fold(y)
        hid[p] = h
        ab[1 + p, body] = (h * jax.nn.sigmoid(h)).astype(BF16)
    act_slices()

    vol_turn(depth, vb[core * (depth + 1), body])
    xv[near_rim] = xvs[core, depth]
    v_rim_mate.start()

    @pl.when(beside_twin)
    def _():
        twin_planes[0][1].wait_recv()
        onward_planes[0][0].start()

    c_from_mate.wait_recv()

    @pl.when((q == 0) & (quad > 0))
    def _():
        c_up.wait_recv()

    @pl.when((q == 3) & (quad < quads - 1))
    def _():
        c_down.wait_recv()

    for p, y in enumerate(outer_part(cg, first, w_turned, mul_turned, agr)):
        h = hid[p]
        s = jax.nn.sigmoid(h)
        hg[core * depth + p, body] = (fold(y) * s * (1.0 + h * (1.0 - s))).astype(BF16)
    h_mate.start()

    def product_of(xs_ref, a, field, lead, count):
        taps = jnp.concatenate(
            [
                jnp.concatenate(
                    [field[lead + p, (2 - b) * pad : (2 - b) * pad + rows] for b in range(3)],
                    axis=1,
                )
                for p in range(count)
            ],
            axis=0,
        )
        return mul(xs_ref[:, a * rows : (a + count) * rows], taps)

    def bit(axis):
        return side if axis == "y" else lax.rem(quad // (1 << axis), 2)

    def partner(axis):
        if axis == "y":
            return across
        return (quad + (1 - 2 * bit(axis)) * (1 << axis)) * 4 + q

    levels = quads.bit_length() - 1
    axes = list(range(levels))[::-1]

    def plan(k):
        order = ORDERS[k] + [axis for axis in range(2, levels)]
        left = (["y"] if k < 3 else []) + axes
        steps, start = [], 0
        for axis in order:
            count = 1 << (len(left) - 1)
            stride = 1 << (len(left) - 1 - left.index(axis))
            steps.append((axis, count, stride, start))
            left.remove(axis)
            start += count
        return steps

    plans = [plan(k) for k in range(6)]

    def place(i, stride, which):
        return i // stride * 2 * stride + which * stride + i % stride

    def hop(k, level):
        axis, count, stride, start = plans[k][level]
        return remote(
            bz.at[k, pl.ds(start, count)], rz.at[k, pl.ds(start, count)],
            sz.at[k, level], qz.at[k, level], partner(axis),
        )

    def give(k, level):
        axis, count, stride, start = plans[k][level]
        for i in range(count):
            bz[k, start + i] = part[k, place(i, stride, 1 - bit(axis))].astype(BF16)
        hop(k, level).start()

    def take(k, level):
        axis, count, stride, start = plans[k][level]
        hop(k, level).wait_recv()
        for i in range(count):
            total = part[k, place(i, stride, bit(axis))] + rz[k, start + i].astype(F32)
            if level + 1 < len(plans[k]):
                part[k, i] = total
            else:
                (g1_ref, g2_ref)[k // 3][9 * (k % 3) : 9 * (k % 3) + 9] = total
        if level + 1 < len(plans[k]):
            give(k, level + 1)

    def first_piece(a):
        term = product_of(xvc, a, hg, 0, duo)
        for i in range(2):
            for z in range(quads):
                for b in range(3):
                    for c in range(3):
                        top = c * half + i * class_chans + z * share
                        part[a, i * quads + z, 3 * b + c] = term[
                            top : top + share, b * chans : (b + 1) * chans
                        ]
        give(a, 0)

    def second_piece(a):
        term = product_of(xtc, a, cg, 1, planes)
        for z in range(quads):
            for b in range(3):
                for c in range(3):
                    top = c * class_chans + z * share
                    part[3 + a, z, 3 * b + c] = term[
                        top : top + share, b * chans : (b + 1) * chans
                    ]
        give(3 + a, 0)

    v_rim_from_mate.wait_recv()
    shift_slices(xv, xvc, (0, duo + 1), half)
    h_from_mate.wait_recv()
    for a in range(3):
        first_piece(a)

    @pl.when(jnp.logical_not(beside_twin))
    def _():
        twin_planes[0][1].wait_recv()
        onward_planes[0][0].start()

    for i in range(1, depth):
        twin_planes[i][1].wait_recv()
        onward_planes[i][0].start()
    act_rims = rims(ab.at[1, body], ab.at[depth, body], ab, as_, ar)
    send_rims(*act_rims)

    shift_slices(xt, xtc, [1 + first + p for p in range(depth)], class_chans)
    slice_from(2, mate).wait_recv()
    shift_slices(xt, xtc, [1 + mate_first + p for p in range(depth)], class_chans)
    take_slices()
    rest = [1 + start + p for start in (twin_first, across_first) for p in range(depth)]
    shift_slices(xt, xtc, rest + [0, planes + 1], class_chans)
    for _, brought in onward_planes:
        brought.wait_recv()
    for a in range(3):
        second_piece(a)
    inner_part(ab, 0, w_second, mul, conv)
    for k, level in TAKES[0]:
        take(k, level)
    take_rims(*act_rims)
    for p, y in enumerate(outer_part(ab, 0, w_second, mul, conv)):
        resp_ref[p] = fold(y).astype(BF16)
    for k, level in TAKES[1]:
        take(k, level)
    for level in range(2, len(plans[0])):
        for k in range(6):
            if (k, level) not in TAKES[1] and level < len(plans[k]):
                take(k, level)

    end_rims(*v_rims)
    end_rims(*act_rims)

    @pl.when(sends_up)
    def _():
        c_up.wait_send()

    @pl.when(sends_down)
    def _():
        c_down.wait_send()

    for to, _ in twin_planes + onward_planes:
        to.wait_send()
    for copy in (c_mate, v_mate, v_rim_mate, h_mate):
        copy.wait_send()
    end_slices()
    for k in range(6):
        for level in range(len(plans[k])):
            hop(k, level).wait_send()


def put(resp, g1, g2, resp_hbm, g1_hbm, g2_hbm, sems):
    pairs = ((resp, resp_hbm), (g1, g1_hbm), (g2, g2_hbm))
    copies = [pltpu.make_async_copy(src, dst, sems.at[i]) for i, (src, dst) in enumerate(pairs)]
    for copy in copies:
        copy.start()
    for copy in copies:
        copy.wait()


def per_device(n, volume, first_filter, second_filter, cotangent):
    depth, width, height, chans = volume.shape
    rows = width * height
    share = chans // n
    quads = n // 4
    planes = 4 * depth
    tall = rows + 2 * height
    class_chans = chans // 4
    levels = quads.bit_length() - 1
    dma = pltpu.SemaphoreType.DMA
    hbm = pl.BlockSpec(memory_space=pl.ANY)
    block = (27, share, chans)
    piece = (9, share, chans)
    vmem = pltpu.VMEM
    response, first, second = pl.pallas_call(
        functools.partial(kernel, n, depth, height),
        out_shape=(
            pltpu.VMEM((depth, rows, chans), BF16),
            pltpu.VMEM(block, F32),
            pltpu.VMEM(block, F32),
        ),
        in_specs=[hbm] * 4,
        out_specs=(pl.BlockSpec(memory_space=pltpu.VMEM),) * 3,
        scratch_shapes=[
            vmem((depth + 2, tall, chans), BF16),
            vmem((depth + 2, tall, chans), BF16),
            vmem((planes + 2, tall, chans), BF16),
            vmem((2 * depth, tall, chans), BF16),
            vmem((27, chans, chans), BF16),
            vmem((27, chans, chans), BF16),
            vmem((depth, rows, 3 * chans), F32),
            vmem((depth, rows, 3 * chans), F32),
            vmem((depth, rows, chans), F32),
            vmem((4, depth, class_chans, rows), BF16),
            vmem((planes + 2, class_chans, rows), BF16),
            vmem((3 * class_chans, (planes + 2) * rows), BF16),
            vmem((2, depth + 1, 2 * class_chans, rows), BF16),
            vmem((2 * depth + 2, 2 * class_chans, rows), BF16),
            vmem((6 * class_chans, (2 * depth + 2) * rows), BF16),
            vmem((6, 2 * quads) + piece, F32),
            vmem((6, 2 * quads) + piece, BF16),
            vmem((6, 2 * quads) + piece, BF16),
            dma((4,)),
            dma((2,)), dma((2,)), dma((2,)), dma((2,)), dma((2,)), dma((2,)),
            dma((depth,)), dma((depth,)), dma((1 + depth,)), dma((1 + depth,)), dma((1,)), dma((1,)),
            dma((3,)), dma((3,)), dma((4,)), dma((2,)), dma((2,)), dma((2,)),
            dma((6, levels + 1)), dma((6, levels + 1)),
        ],
        compiler_params=pltpu.CompilerParams(
            collective_id=0, has_side_effects=True, vmem_limit_bytes=58 * 1024 * 1024
        ),
    )(
        volume.reshape(depth, rows, chans),
        first_filter.reshape(27, chans, chans),
        second_filter.reshape(27, chans, chans),
        cotangent.reshape(depth, rows, chans),
    )
    response, first, second = pl.pallas_call(
        put,
        out_shape=(
            jax.ShapeDtypeStruct((depth, rows, chans), BF16),
            jax.ShapeDtypeStruct(block, F32),
            jax.ShapeDtypeStruct(block, F32),
        ),
        in_specs=[pl.BlockSpec(memory_space=pltpu.VMEM)] * 3,
        out_specs=(hbm,) * 3,
        scratch_shapes=[dma((3,))],
    )(*(pltpu.with_memory_space_constraint(x, pltpu.VMEM) for x in (response, first, second)))

    def laid(grad):
        return jnp.transpose(grad, (1, 0, 2)).reshape(share, 3, 3, 3, chans)

    return response.reshape(volume.shape), laid(first), laid(second)


def solution(mesh):
    n = mesh.shape["space"]
    field = P(("parts", "space"), None, None, None)
    grad = P(("parts", "space"), None, None, None, None)
    return jax.shard_map(
        functools.partial(per_device, n),
        mesh=mesh,
        in_specs=(field, P(), P(), field),
        out_specs=(field, grad, grad),
        check_vma=False,
    )
```
